32 devices in a mesh: grp: 2 (over y), row: 4 (over z), head: 2 (over x), br: 2 (over core).
Axes of the slice: x: 2, y: 2, z: 4, core: 2. Of those that a mesh axis runs over, the one named last changes fastest.
Arguments:
- pair_acts: float32 [16, 8, 128], P(('grp', 'row', 'head')), parts along dimension 0, may hold values from -6 to 6
- alignment: float32 [64, 8, 256], P(('grp', 'br'), ('row', 'head')), parts along dimension 0, may hold values from -6 to 6
- align_mask: int32 [64, 8], P('grp', ('row', 'head')), parts along dimension 0, may hold values from 0 to 1
- residue_mask: int32 [16], P('grp'), parts along dimension 0, may hold values from 0 to 1, as said below
- align_gain: float32 [256], replicated, may hold values from 0.25 to 1.75
- outer_in: float32 [256, 64], replicated, may hold values from -0.375 to 0.375
- outer_out: float32 [1024, 128], replicated, may hold values from -1 to 1
- tri_gain: float32 [2, 128], replicated, may hold values from 0.25 to 1.75
- tri_in: float32 [2, 128, 4, 128], P(None, None, 'br'), may hold values from -5 to 5
- tri_bias: float32 [2, 128, 4], P(None, None, 'br'), may hold values from -0.5 to 0.5
- tri_out: float32 [2, 4, 32, 128], P(None, 'br'), may hold values from -0.5 to 0.5
- pair_cotangent: float32 [16, 8, 128], P(('grp', 'row', 'head')), parts along dimension 0, may hold values from -6 to 6
Outputs:
- pair_out: float32 [16, 8, 128], P(('grp', 'row', 'head')), parts along dimension 0
- pair_grad: float32 [16, 8, 128], P(('grp', 'row', 'head')), parts along dimension 0
The draws below stay inside these ranges and needn't reach their ends.
There are 2 independent parts, one for each index of `grp`. The reference program is written for one: setup_inputs(seed, part) draws one part's arguments, and reference() takes and returns one part's arrays. A program takes and returns all parts, laid end to end along the dimension named above; an argument that names none is the same for every part. Nothing has to cross between parts.
Inputs may be any that keep to these rules, and one draw needn't show every extreme that they name: `residue_mask`: 1 at residue 0, and 0 at one or more residues; `align_mask`: 1 at every residue of sequence 0 of each part.
All inputs are finite; a program needn't handle non-finite values.
Results may differ from the reference program's by a relative error of at most 0.0003.
Values sent between devices are 32-bit elements; how exact they have to be, the bound alone decides.
A program may use at most 64 MiB of HBM per device.

```python
import jax
import jax.numpy as jnp
from jax import lax

C = 128
CM = 256
OPC = 32
HEADS = 4
HD = 32
N = 8
S = 32


def draw_align_mask(key, part):
    draws_int = jax.random.randint(key, (S, N), 0, 4)
    leading = jnp.arange(S)[:, None] == 0
    return jnp.where(leading, 1, jnp.minimum(draws_int, 1)).astype(jnp.int32)


def draw_residue_mask(key, part):
    first_key = jax.random.fold_in(key, 11)
    second_key = jax.random.fold_in(key, 23)
    draws_int = jax.random.randint(first_key, (N,), 0, 4)
    dropped = jax.random.randint(second_key, (), 1, N)
    places = jnp.arange(N)
    values = jnp.minimum(draws_int, 1)
    values = jnp.where(places == 0, 1, values)
    values = jnp.where(places == dropped, 0, values)
    return values.astype(jnp.int32)


def draw_tri_in(key, part):
    weights = jax.random.truncated_normal(key, -4.0, 4.0, (2, C, HEADS, 4 * HD), jnp.float32) * C ** (-0.5)
    return weights


def shard_levels(own_key, dims, pieces, smallest, largest):
    def one(axis_at, shards_of):
        draws = jax.random.uniform(jax.random.fold_in(jax.random.fold_in(own_key, 6), axis_at), (shards_of,), jnp.float32, smallest / len(pieces), largest / len(pieces))
        return jnp.repeat(jnp.exp(draws), dims[axis_at] // shards_of).reshape((-1,) + (1,) * (len(dims) - axis_at - 1))

    gain = one(*pieces[0])
    for cut in pieces[1:]:
        gain = gain * one(*cut)
    return gain


def gaussian(own_key, dims, scale, most, split=(), dtype=jnp.bfloat16):
    entries = jax.random.normal(own_key, dims, jnp.float32) * scale
    if len(split) > 0:
        entries = shard_levels(own_key, dims, split, -0.22, 0.18) * entries
    return jnp.clip(entries, min=-most, max=most).astype(dtype)


def setup_inputs(seed: int = 0, part: int = 0) -> dict:
    keys = jax.random.split(jax.random.key(seed), 13)
    own_keys = jax.random.split(jax.random.fold_in(keys[12], part), 13)
    pair_acts = gaussian(own_keys[0], (N, N, C), 1.0, 6.0, ((0, 8),), jnp.float32)
    alignment = gaussian(own_keys[1], (S, N, CM), 1.0, 6.0, ((0, 2), (1, 8)), jnp.float32)
    align_mask = draw_align_mask(jax.random.fold_in(jax.random.fold_in(keys[12], part), 71), part)
    residue_mask = draw_residue_mask(jax.random.fold_in(jax.random.fold_in(keys[12], part), 71), part)
    align_gain = jnp.clip(1.0 + 0.15 * jax.random.normal(keys[4], (CM,), jnp.float32), 0.25, 1.75)
    outer_in = gaussian(keys[5], (CM, 2 * OPC), CM ** -0.5, 0.375, (), jnp.float32)
    outer_out = gaussian(keys[6], (OPC * OPC, C), OPC ** -0.5, 1.0, (), jnp.float32)
    tri_gain = jnp.clip(1.0 + 0.15 * jax.random.normal(keys[7], (2, C), jnp.float32), 0.25, 1.75)
    tri_in = draw_tri_in(jax.random.fold_in(keys[12], 71), part)
    tri_bias = gaussian(keys[9], (2, C, HEADS), C ** -0.5, 0.5, ((2, 2),), jnp.float32)
    tri_out = gaussian(keys[10], (2, HEADS, HD, C), (HEADS * HD) ** -0.5, 0.5, ((1, 2),), jnp.float32)
    pair_cotangent = gaussian(own_keys[11], (N, N, C), 1.0, 6.0, ((0, 8),), jnp.float32)
    return dict(pair_acts=pair_acts, alignment=alignment, align_mask=align_mask, residue_mask=residue_mask, align_gain=align_gain, outer_in=outer_in, outer_out=outer_out, tri_gain=tri_gain, tri_in=tri_in, tri_bias=tri_bias, tri_out=tri_out, pair_cotangent=pair_cotangent)


PRECISE = lax.Precision.HIGHEST
EPSILON = 1e-05
MASK_SHIFT = 1000000000.0

def normalize(values, scales):
    average = lax.optimization_barrier(jnp.mean(values, axis=-1, keepdims=True))
    centred = values - average
    spread = lax.optimization_barrier(jnp.mean(centred * centred, axis=-1, keepdims=True))
    return centred * lax.rsqrt(spread + EPSILON) * scales

def outer_update(alignment, align_mask, align_gain, outer_in, outer_out):
    mask_all = align_mask.astype(jnp.float32)
    normed = normalize(alignment, align_gain)
    projected = jnp.einsum('snc,ck->snk', normed, outer_in, precision=PRECISE)
    left_part = projected[..., :OPC] * mask_all[..., None]
    right_part = projected[..., OPC:] * mask_all[..., None]
    table = outer_out.reshape(OPC, OPC, C)
    mixed_left = jnp.einsum('sip,pqc->siqc', left_part, table, precision=PRECISE)
    summed = jnp.einsum('siqc,sjq->ijc', mixed_left, right_part, precision=PRECISE)
    counts = jnp.einsum('si,sj->ij', mask_all, mask_all, precision=PRECISE)
    return summed / counts[..., None]

def row_attention(rows_in, live, scales, weight_in, weight_bias, weight_out):
    normed = normalize(rows_in, scales)
    projected = jnp.einsum('ijc,chd->ijhd', normed, weight_in, precision=PRECISE)
    bias_full = jnp.einsum('jkc,ch->hjk', normed, weight_bias, precision=PRECISE)
    key_shift = (live - 1.0) * MASK_SHIFT
    scale_factor = HD ** (-0.5)

    def one_row(carried):
        row_proj, row_flag = carried
        queries = row_proj[:, :, :HD]
        key_proj = row_proj[:, :, HD:2 * HD]
        value_proj = row_proj[:, :, 2 * HD:3 * HD]
        gating = row_proj[:, :, 3 * HD:]
        logits = jnp.einsum('jhd,khd->hjk', queries, key_proj, precision=PRECISE) * scale_factor
        logits = logits + bias_full + key_shift
        attention = jax.nn.softmax(logits, axis=-1)
        attended = jnp.einsum('hjk,khd->jhd', attention, value_proj, precision=PRECISE)
        gated_out = jax.nn.sigmoid(gating) * attended
        update = jnp.einsum('jhd,hdc->jc', gated_out, weight_out, precision=PRECISE)
        return update * (row_flag * live)[:, None]
    updates = lax.map(one_row, (projected, live))
    return rows_in + updates

def reference(pair_acts, alignment, align_mask, residue_mask, align_gain, outer_in, outer_out, tri_gain, tri_in, tri_bias, tri_out, pair_cotangent):
    live = residue_mask.astype(jnp.float32)
    outer = outer_update(alignment, align_mask, align_gain, outer_in, outer_out)

    def forward(values):
        pair_one = values + outer
        pair_two = row_attention(pair_one, live, tri_gain[0], tri_in[0], tri_bias[0], tri_out[0])
        turned = row_attention(jnp.swapaxes(pair_two, 0, 1), live, tri_gain[1], tri_in[1], tri_bias[1], tri_out[1])
        return jnp.swapaxes(turned, 0, 1)
    pair_out, pull_back = jax.vjp(forward, pair_acts)
    pair_grad, = pull_back(pair_cotangent)
    return (pair_out, pair_grad)
```

```python
import functools

import jax
import jax.numpy as jnp
from jax import lax
from jax.experimental import pallas as pl
from jax.experimental.pallas import tpu as pltpu
from jax.sharding import PartitionSpec as P

OPC = 32


PRECISE = lax.Precision.HIGHEST
EPSILON = 1e-05
MASK_SHIFT = 1000000000.0


def normalize(values, scales):
    average = jnp.mean(values, axis=-1, keepdims=True)
    centred = values - average
    spread = jnp.mean(centred * centred, axis=-1, keepdims=True)
    return centred * lax.rsqrt(spread + EPSILON) * scales


def core_total(values):
    return lax.psum(values, "br")


def reorient(values):
    turned = jnp.swapaxes(values, 0, 1)
    return lax.all_to_all(turned, ("row", "head"), split_axis=0, concat_axis=1, tiled=True)


def prepare(values, scales, weight_in, weight_bias):
    normed = normalize(values, scales)
    projected = jnp.einsum("ijc,chd->ijhd", normed, weight_in, precision=PRECISE)
    bias_local = jnp.einsum("jkc,ch->hjk", normed, weight_bias, precision=PRECISE)
    return (projected, bias_local)


def attend(projected, bias_full, key_shift, weight_out):
    head_size = projected.shape[-1] // 4
    queries = projected[..., :head_size]
    key_proj = projected[..., head_size : 2 * head_size]
    value_proj = projected[..., 2 * head_size : 3 * head_size]
    gating = projected[..., 3 * head_size :]
    logits = jnp.einsum("ijhd,ikhd->ihjk", queries, key_proj, precision=PRECISE) * head_size ** (
        -0.5
    )
    logits = logits + bias_full[None] + key_shift
    attention = jax.nn.softmax(logits, axis=-1)
    attended = jnp.einsum("ihjk,ikhd->ijhd", attention, value_proj, precision=PRECISE)
    gated_out = jax.nn.sigmoid(gating) * attended
    return jnp.einsum("ijhd,hdc->ijc", gated_out, weight_out, precision=PRECISE)


def tri_forward(rows_in, scales, weight_in, weight_bias, weight_out, key_shift, pair_mask):

    def local_prep(values):
        return prepare(values, scales, weight_in, weight_bias)

    (projected, bias_local), pull_prep = jax.vjp(local_prep, rows_in)
    bias_full = lax.all_gather(bias_local, ("row", "head"), axis=1, tiled=True)

    def local_attend(proj_in, bias_in):
        return attend(proj_in, bias_in, key_shift, weight_out)

    partial_out, pull_attend = jax.vjp(local_attend, projected, bias_full)
    total_out = core_total(partial_out)
    return (rows_in + total_out * pair_mask, (pull_prep, pull_attend))


def tri_backward(grad_out, saved, pair_mask):
    pull_prep, pull_attend = saved
    grad_proj, grad_bias = pull_attend(grad_out * pair_mask)
    grad_local = lax.psum_scatter(grad_bias, ("row", "head"), scatter_dimension=1, tiled=True)
    (grad_rows,) = pull_prep((grad_proj, grad_local))
    return grad_out + core_total(grad_rows)


def spread_body(
    pair_acts,
    alignment,
    align_mask,
    residue_mask,
    align_gain,
    outer_in,
    outer_out,
    tri_gain,
    tri_in,
    tri_bias,
    tri_out,
    pair_cotangent,
):
    row_count = pair_acts.shape[0]
    live = residue_mask.astype(jnp.float32)
    key_shift = (live - 1.0) * MASK_SHIFT
    row_live = lax.dynamic_slice_in_dim(
        live, lax.axis_index(("row", "head")) * row_count, row_count, 0
    )
    pair_mask = row_live[:, None, None] * live[None, :, None]
    seq_count = alignment.shape[0]
    mask_all = align_mask.astype(jnp.float32)
    mask_own = lax.dynamic_slice_in_dim(mask_all, lax.axis_index("br") * seq_count, seq_count, 0)
    normed = normalize(alignment, align_gain)
    projected = jnp.einsum("snc,ck->snk", normed, outer_in, precision=PRECISE)
    left_part = projected[..., :OPC] * mask_own[..., None]
    right_part = jnp.swapaxes(projected[..., OPC:] * mask_own[..., None], 1, 2)
    right_all, mask_cols = (
        lax.all_gather(right_part, ("row", "head"), axis=2, tiled=True),
        lax.all_gather(mask_all, ("row", "head"), axis=1, tiled=True),
    )
    counts = jnp.einsum("si,sj->ij", mask_all, mask_cols, precision=PRECISE)
    table = outer_out.reshape(OPC, OPC, outer_out.shape[-1])
    mixed_left = jnp.einsum("sip,pqc->siqc", left_part, table, precision=PRECISE)
    partial_outer = jnp.einsum("siqc,sqj->ijc", mixed_left, right_all, precision=PRECISE)
    outer_sum = core_total(partial_outer)
    pair_one = pair_acts + outer_sum / counts[..., None]
    pair_two, saved_start = tri_forward(
        pair_one, tri_gain[0], tri_in[0], tri_bias[0], tri_out[0], key_shift, pair_mask
    )
    turned_two = reorient(pair_two)
    turned_three, saved_end = tri_forward(
        turned_two, tri_gain[1], tri_in[1], tri_bias[1], tri_out[1], key_shift, pair_mask
    )
    pair_out = reorient(turned_three)
    grad_turned = reorient(pair_cotangent)
    grad_turned = tri_backward(grad_turned, saved_end, pair_mask)
    grad_two = reorient(grad_turned)
    pair_grad = tri_backward(grad_two, saved_start, pair_mask)
    return (pair_out, pair_grad)


MESH_ID = pl.DeviceIdType.MESH
FUSED_BYTES = 1 << 20
NN = ((1,), (0,))
NT = ((1,), (1,))
TN = ((0,), (0,))


def split(values):
    high = values.astype(jnp.bfloat16)
    low = (values - high.astype(jnp.float32)).astype(jnp.bfloat16)
    return (high, low)


def pair_dot(first, second, dims):
    def one(a, b):
        return lax.dot_general(a, b, (dims, ((), ())), preferred_element_type=jnp.float32)

    return one(first[0], second[0]) + (one(first[0], second[1]) + one(first[1], second[0]))


def standardize(values):
    average = jnp.mean(values, axis=-1, keepdims=True)
    centred = values - average
    spread = jnp.mean(centred * centred, axis=-1, keepdims=True)
    inverse = lax.rsqrt(spread + EPSILON)
    return (centred * inverse, inverse)


def fused_kernel(
    sizes,
    live_ref,
    acts_hbm,
    align_hbm,
    mask_hbm,
    gain_hbm,
    outer_in_hbm,
    outer_out_hbm,
    tri_gain_hbm,
    tri_in_hbm,
    tri_bias_hbm,
    tri_out_hbm,
    cot_hbm,
    out_ref,
    grad_ref,
    acts_all,
    cot_all,
    proj_all,
    align_v,
    mask_v,
    gain_v,
    outer_in_v,
    outer_out_v,
    tri_gain_v,
    tri_in_all,
    tri_bias_all,
    tri_out_all,
    table_hi,
    table_lo,
    wide_hi,
    wide_lo,
    turn_v,
    mixed_v,
    load_sems,
    send_acts,
    recv_acts,
    send_proj,
    recv_proj,
    send_cot,
    recv_cot,
    send_w,
    recv_w,
):
    rows_n, heads_n, cores_n = sizes
    count = rows_n * heads_n
    chan = acts_all.shape[-1]
    my_row = lax.axis_index("row")
    my_head = lax.axis_index("head")
    my_core = lax.axis_index("br")
    me = my_row * heads_n + my_head
    seqs = align_v.shape[0]
    half = tri_in_all.shape[3]
    head_count = half * cores_n
    size = tri_in_all.shape[4] // 4
    width = head_count * size

    peers = [
        (dr, dh, db)
        for dr in range(rows_n)
        for dh in range(heads_n)
        for db in range(cores_n)
        if (dr, dh, db) != (0, 0, 0)
    ]

    def place(offset):
        dr, dh, db = offset
        return (
            lax.rem(my_row + dr, rows_n),
            lax.rem(my_head + dh, heads_n),
            lax.rem(my_core + db, cores_n),
        )

    def target(offset):
        row, head, core = place(offset)
        return {"row": row, "head": head, "br": core}

    barrier = pltpu.get_barrier_semaphore()
    for offset in peers:
        pl.semaphore_signal(barrier, inc=1, device_id=target(offset), device_id_type=MESH_ID)

    loads = [
        pltpu.make_async_copy(align_hbm, align_v, load_sems.at[0]),
        pltpu.make_async_copy(gain_hbm, gain_v, load_sems.at[1]),
        pltpu.make_async_copy(outer_in_hbm, outer_in_v, load_sems.at[2]),
        pltpu.make_async_copy(mask_hbm, mask_v, load_sems.at[3]),
        pltpu.make_async_copy(acts_hbm.at[0], acts_all.at[me, 0:count], load_sems.at[4]),
        pltpu.make_async_copy(tri_in_hbm, tri_in_all.at[my_core], load_sems.at[5]),
        pltpu.make_async_copy(tri_bias_hbm, tri_bias_all.at[my_core], load_sems.at[6]),
        pltpu.make_async_copy(tri_out_hbm, tri_out_all.at[my_core], load_sems.at[7]),
        pltpu.make_async_copy(cot_hbm.at[0], cot_all.at[me], load_sems.at[8]),
        pltpu.make_async_copy(outer_out_hbm, outer_out_v, load_sems.at[9]),
        pltpu.make_async_copy(tri_gain_hbm, tri_gain_v, load_sems.at[10]),
    ]
    for load in loads:
        load.start()
    for load in loads[:4]:
        load.wait()

    aligned = align_v[:, 0, :]
    normed = standardize(aligned)[0] * gain_v[...]
    projected = pair_dot(split(normed), split(outer_in_v[...]), NN)
    mask_f = mask_v[...].astype(jnp.float32)
    lo_seq = mask_f[0:seqs]
    mask_own = lo_seq
    for core in range(1, cores_n):
        mask_own = jnp.where(my_core == core, mask_f[core * seqs : (core + 1) * seqs], mask_own)
    projected = projected * mask_own
    pieces = seqs // 8
    proj_all[my_core, me] = jnp.concatenate(
        [projected[8 * piece : 8 * piece + 8] for piece in range(pieces)], axis=1
    )
    depth = mask_f.shape[0]
    lane = lax.broadcasted_iota(jnp.int32, (depth, chan), 1)
    place_s = lax.broadcasted_iota(jnp.int32, (depth, chan), 0)
    mask_row = jnp.sum(jnp.where(lane == place_s, mask_f, 0.0), axis=0, keepdims=True)
    acts_all[me, count : count + 1] = mask_row
    for load in loads[4:]:
        load.wait()

    pl.semaphore_wait(barrier, len(peers))

    sends = []
    receives = []
    weight_receives = []
    cot_receives = []

    def remote(src, dst, send_sem, recv_sem, offset):
        return pltpu.make_async_remote_copy(
            src_ref=src,
            dst_ref=dst,
            send_sem=send_sem,
            recv_sem=recv_sem,
            device_id=target(offset),
            device_id_type=MESH_ID,
        )

    ordered = sorted(peers, key=lambda o: -(min(o[0], rows_n - o[0]) + o[1]))
    for number, offset in enumerate(ordered):
        row, head, core = place(offset)
        other = row * heads_n + head
        copy = remote(
            proj_all.at[my_core, me],
            proj_all.at[my_core, me],
            send_proj.at[number],
            recv_proj.at[my_core, me],
            offset,
        )
        copy.start()
        sends.append(copy)
        receives.append(
            remote(
                proj_all.at[core, other],
                proj_all.at[core, other],
                send_proj.at[number],
                recv_proj.at[core, other],
                offset,
            )
        )
        if offset[2] == 0:
            copy = remote(
                acts_all.at[me, 0 : count + 1],
                acts_all.at[me, 0 : count + 1],
                send_acts.at[number],
                recv_acts.at[me],
                offset,
            )
            copy.start()
            sends.append(copy)
            receives.append(
                remote(
                    acts_all.at[other, 0 : count + 1],
                    acts_all.at[other, 0 : count + 1],
                    send_acts.at[number],
                    recv_acts.at[other],
                    offset,
                )
            )
    for db in range(1, cores_n):
        offset = (0, 0, db)
        core = lax.rem(my_core + db, cores_n)
        for which, ref in enumerate((tri_in_all, tri_bias_all, tri_out_all)):
            copy = remote(
                ref.at[my_core],
                ref.at[my_core],
                send_w.at[which, db],
                recv_w.at[which, my_core],
                offset,
            )
            copy.start()
            sends.append(copy)
            weight_receives.append(
                remote(
                    ref.at[core],
                    ref.at[core],
                    send_w.at[which, db],
                    recv_w.at[which, core],
                    offset,
                )
            )
    for number, offset in enumerate(ordered):
        if offset[2] == 0:
            row, head, core = place(offset)
            other = row * heads_n + head
            copy = remote(
                cot_all.at[me], cot_all.at[me], send_cot.at[number], recv_cot.at[me], offset
            )
            copy.start()
            sends.append(copy)
            cot_receives.append(
                remote(
                    cot_all.at[other],
                    cot_all.at[other],
                    send_cot.at[number],
                    recv_cot.at[other],
                    offset,
                )
            )

    for q in range(OPC):
        high, low = split(outer_out_v[pl.ds(q, OPC, stride=OPC), :])
        table_hi[q * OPC : (q + 1) * OPC] = high
        table_lo[q * OPC : (q + 1) * OPC] = low

    pairs = count * count
    lanes = head_count * pairs
    tile_row = lax.broadcasted_iota(jnp.int32, (count, count, lanes), 0)
    lane_at = lax.rem(lax.broadcasted_iota(jnp.int32, (count, count, lanes), 2), pairs)
    at_first = tile_row == lane_at // count
    at_second = tile_row == lax.rem(lane_at, count)
    live = [live_ref[n].astype(jnp.float32) for n in range(count)]
    key_at = lax.broadcasted_iota(jnp.int32, (count, lanes), 0)
    first_at = lax.broadcasted_iota(jnp.int32, (count, count, chan), 0)
    second_at = lax.broadcasted_iota(jnp.int32, (count, count, chan), 1)
    key_live = jnp.zeros((count, lanes), jnp.float32)
    live_first = jnp.zeros((count, count, chan), jnp.float32)
    live_second = jnp.zeros((count, count, chan), jnp.float32)
    for n in range(count):
        key_live = jnp.where(key_at == n, live[n], key_live)
        live_first = jnp.where(first_at == n, live[n], live_first)
        live_second = jnp.where(second_at == n, live[n], live_second)
    key_shift = (key_live - 1.0) * MASK_SHIFT
    pair_mask = (live_first * live_second).reshape(pairs, chan)
    lane_head = lax.broadcasted_iota(jnp.int32, (pairs, width), 1) // size

    def heads_apart(values):
        return jnp.concatenate(
            [jnp.where(lane_head == h, values, 0.0) for h in range(head_count)], axis=0
        )

    def heads_together(values):
        total = jnp.where(lane_head == 0, values[0:pairs], 0.0)
        for h in range(1, head_count):
            total = jnp.where(lane_head == h, values[h * pairs : (h + 1) * pairs], total)
        return total

    def spread_over(values, where):
        return jnp.where(where, values[None], 0.0).reshape(pairs, lanes)

    def fold(values, where):
        return jnp.sum(jnp.where(where, values.reshape(count, count, lanes), 0.0), axis=0)

    for receive in weight_receives:
        receive.wait_recv()

    outs = []
    for t in range(2):
        blocks = []
        for h in range(head_count):
            blocks.append(tri_in_all[h // half, t, :, h % half, :])
        for block in range(4):
            columns = jnp.concatenate(
                [b[:, block * size : (block + 1) * size] for b in blocks], axis=1
            )
            high, low = split(columns)
            wide_hi[t, :, block * width : (block + 1) * width] = high
            wide_lo[t, :, block * width : (block + 1) * width] = low
        bias_columns = jnp.concatenate(
            [
                jnp.broadcast_to(
                    tri_bias_all[h // half, t, :, h % half : h % half + 1], (chan, pairs)
                )
                for h in range(head_count)
            ],
            axis=1,
        )
        high, low = split(bias_columns)
        wide_hi[t, :, 4 * width :] = high
        wide_lo[t, :, 4 * width :] = low
        outs.append(
            split(
                jnp.concatenate(
                    [tri_out_all[h // half, t, h % half] for h in range(head_count)], axis=0
                )
            )
        )

    for receive in receives:
        receive.wait_recv()

    left_tiles = []
    right_tiles = []
    for core in range(cores_n):
        for piece in range(pieces):
            base = piece * 2 * OPC
            left_tiles.append(
                jnp.concatenate(
                    [proj_all[core, n, :, base : base + OPC] for n in range(count)], axis=1
                )
            )
            right_tiles.append(
                jnp.concatenate(
                    [proj_all[core, n, :, base + OPC : base + 2 * OPC] for n in range(count)],
                    axis=1,
                )
            )
    left = jnp.concatenate(left_tiles, axis=0)
    right = jnp.concatenate(right_tiles, axis=0)
    mixed = pair_dot(split(right), split(left), TN)
    for block in range(mixed_v.shape[0]):
        mixed_v[block] = mixed[:, block * chan : (block + 1) * chan]
    strips = [[] for _ in range(count)]
    for q in range(OPC):
        for block in range(mixed_v.shape[0]):
            tile = mixed_v[block, pl.ds(q, count, stride=OPC), :]
            for n in range(chan // OPC):
                strips[block * (chan // OPC) + n].append(tile[:, n * OPC : (n + 1) * OPC])
    crossed = jnp.concatenate([jnp.concatenate(s, axis=1) for s in strips], axis=0)
    summed = pair_dot(split(crossed), (table_hi[...], table_lo[...]), NN)
    mask_rows = jnp.concatenate([acts_all[n, count : count + 1] for n in range(count)], axis=0)
    counts = jnp.sum(mask_rows[:, None, :] * mask_rows[None, :, :], axis=-1, keepdims=True)
    acts = jnp.concatenate([acts_all[n, 0:count] for n in range(count)], axis=0)
    pair_one = acts + summed / counts.reshape(pairs, 1)

    def turn(values):
        turn_v[...] = values
        return jnp.concatenate(
            [turn_v[pl.ds(n, count, stride=count), :] for n in range(count)], axis=0
        )

    scale = size ** (-0.5)

    def forward(x, t):
        gain = tri_gain_v[t : t + 1]
        hat, inverse = standardize(x)
        weights = (wide_hi[t], wide_lo[t])
        projected = pair_dot(split(hat * gain), weights, NN)
        query = projected[:, 0:width] * scale
        key = split(projected[:, width : 2 * width])
        value = split(projected[:, 2 * width : 3 * width])
        gate = jax.nn.sigmoid(projected[:, 3 * width : 4 * width])
        bias = fold(projected[:, 4 * width :], at_second)
        query_apart = split(heads_apart(query))
        logits = fold(pair_dot(key, query_apart, NT), at_first) + bias + key_shift
        top = jnp.max(logits, axis=0, keepdims=True)
        exps = jnp.exp(logits - top)
        probs = exps / jnp.sum(exps, axis=0, keepdims=True)
        probs_wide = split(spread_over(probs, at_first))
        attended = heads_together(pair_dot(probs_wide, value, TN))
        update = pair_dot(split(gate * attended), outs[t], NN)
        saved = (hat, inverse, gain, weights, key, value, gate, query_apart, probs, probs_wide, attended)
        return (x + update * pair_mask, saved)

    def backward(grad, t, saved):
        hat, inverse, gain, weights, key, value, gate, query_apart, probs, probs_wide, attended = saved
        d_gated = pair_dot(split(grad * pair_mask), outs[t], NT)
        d_gate = d_gated * attended * gate * (1.0 - gate)
        d_apart = split(heads_apart(d_gated * gate))
        d_probs = fold(pair_dot(value, d_apart, NT), at_first)
        d_value = pair_dot(probs_wide, d_apart, NN)
        d_logits = probs * (d_probs - jnp.sum(probs * d_probs, axis=0, keepdims=True))
        d_wide = split(spread_over(d_logits, at_first))
        d_key = pair_dot(d_wide, query_apart, NN)
        d_query = heads_together(pair_dot(d_wide, key, TN)) * scale
        d_bias = spread_over(d_logits, at_second)
        d_all = jnp.concatenate([d_query, d_key, d_value, d_gate, d_bias], axis=1)
        d_normed = pair_dot(split(d_all), weights, NT) * gain
        mean_d = jnp.mean(d_normed, axis=-1, keepdims=True)
        mean_dh = jnp.mean(d_normed * hat, axis=-1, keepdims=True)
        return grad + inverse * (d_normed - mean_d - hat * mean_dh)

    pair_two, saved_start = forward(pair_one, 0)
    turned, saved_end = forward(turn(pair_two), 1)
    turn_v[...] = turned
    out_ref[0] = turn_v[pl.ds(me, count, stride=count), :]

    for receive in cot_receives:
        receive.wait_recv()
    cot = jnp.concatenate(
        [cot_all[:, n, :] for n in range(count)], axis=0
    )
    grad_two = turn(backward(cot, 1, saved_end))
    turn_v[...] = backward(grad_two, 0, saved_start)
    grad_ref[0] = turn_v[pl.ds(pl.multiple_of(me * count, count), count), :]

    for copy in sends:
        copy.wait_send()


def fused_body(shape, args):
    (
        pair_acts,
        alignment,
        align_mask,
        residue_mask,
        align_gain,
        outer_in,
        outer_out,
        tri_gain,
        tri_in,
        tri_bias,
        tri_out,
        pair_cotangent,
    ) = args
    rows_n, heads_n, cores_n = shape["row"], shape["head"], shape["br"]
    count = rows_n * heads_n
    chan = pair_acts.shape[-1]
    seqs = alignment.shape[0]
    half, size = tri_in.shape[2], tri_in.shape[3] // 4
    head_count = half * cores_n
    lanes = head_count * count * count
    wide = 4 * head_count * size + lanes
    others = count * cores_n
    f32, b16 = jnp.float32, jnp.bfloat16
    anywhere = pl.BlockSpec(memory_space=pl.ANY)
    here = pl.BlockSpec(memory_space=pltpu.VMEM)
    dma = pltpu.SemaphoreType.DMA
    scratch = [
        pltpu.VMEM((count, count + 8, chan), f32),
        pltpu.VMEM((count, count, chan), f32),
        pltpu.VMEM((cores_n, count, 8, (seqs // 8) * 2 * OPC), f32),
        pltpu.VMEM(alignment.shape, f32),
        pltpu.VMEM(align_mask.shape, jnp.int32),
        pltpu.VMEM((1, align_gain.shape[0]), f32),
        pltpu.VMEM(outer_in.shape, f32),
        pltpu.VMEM(outer_out.shape, f32),
        pltpu.VMEM(tri_gain.shape, f32),
        pltpu.VMEM((cores_n,) + tri_in.shape, f32),
        pltpu.VMEM((cores_n,) + tri_bias.shape, f32),
        pltpu.VMEM((cores_n,) + tri_out.shape, f32),
        pltpu.VMEM(outer_out.shape, b16),
        pltpu.VMEM(outer_out.shape, b16),
        pltpu.VMEM((2, chan, wide), b16),
        pltpu.VMEM((2, chan, wide), b16),
        pltpu.VMEM((count * count, chan), f32),
        pltpu.VMEM((count * OPC // chan, count * OPC, chan), f32),
        dma((11,)),
        dma((others,)),
        dma((count,)),
        dma((others,)),
        dma((cores_n, count)),
        dma((others,)),
        dma((count,)),
        dma((3, cores_n)),
        dma((3, cores_n)),
    ]
    return pl.pallas_call(
        functools.partial(fused_kernel, (rows_n, heads_n, cores_n)),
        out_shape=(
            jax.ShapeDtypeStruct(pair_acts.shape, f32),
            jax.ShapeDtypeStruct(pair_acts.shape, f32),
        ),
        in_specs=[pl.BlockSpec(memory_space=pltpu.SMEM)] + [anywhere] * 11,
        out_specs=(here, here),
        scratch_shapes=scratch,
        compiler_params=pltpu.CompilerParams(collective_id=0, has_side_effects=True),
    )(
        residue_mask,
        pair_acts,
        alignment,
        align_mask,
        align_gain[None],
        outer_in,
        outer_out,
        tri_gain,
        tri_in,
        tri_bias,
        tri_out,
        pair_cotangent,
    )


def dispatch(shape, *args):
    pair_acts, alignment, align_mask, tri_in = args[0], args[1], args[2], args[8]
    count = pair_acts.shape[1]
    head_count = tri_in.shape[2] * shape["br"]
    chan = pair_acts.shape[-1]
    fits = (
        pair_acts.shape[0] == 1
        and alignment.shape[1] == 1
        and count % 8 == 0
        and alignment.shape[0] % 8 == 0
        and align_mask.shape[0] <= chan
        and head_count * (tri_in.shape[3] // 4) == chan
        and head_count * count**4 * 4 <= FUSED_BYTES
    )
    return fused_body(shape, args) if fits else spread_body(*args)


def solution(mesh):
    in_specs = (
        P(("grp", "row", "head"), None, None),
        P(("grp", "br"), ("row", "head"), None),
        P("grp", ("row", "head")),
        P("grp"),
        P(),
        P(),
        P(),
        P(),
        P(None, None, "br", None),
        P(None, None, "br"),
        P(None, "br", None, None),
        P(("grp", "row", "head"), None, None),
    )
    out_specs = (P(("grp", "row", "head"), None, None), P(("grp", "row", "head"), None, None))
    return jax.shard_map(functools.partial(dispatch, dict(mesh.shape)), mesh=mesh, in_specs=in_specs, out_specs=out_specs, check_vma=False)
```

```python
import functools

import jax
import jax.numpy as jnp
from jax import lax
from jax.experimental import pallas as pl
from jax.experimental.pallas import tpu as pltpu
from jax.sharding import PartitionSpec as P

OPC = 32


PRECISE = lax.Precision.HIGHEST
EPSILON = 1e-05
MASK_SHIFT = 1000000000.0


def normalize(values, scales):
    average = jnp.mean(values, axis=-1, keepdims=True)
    centred = values - average
    spread = jnp.mean(centred * centred, axis=-1, keepdims=True)
    return centred * lax.rsqrt(spread + EPSILON) * scales


def core_total(values):
    return lax.psum(values, "br")


def reorient(values):
    turned = jnp.swapaxes(values, 0, 1)
    return lax.all_to_all(turned, ("row", "head"), split_axis=0, concat_axis=1, tiled=True)


def prepare(values, scales, weight_in, weight_bias):
    normed = normalize(values, scales)
    projected = jnp.einsum("ijc,chd->ijhd", normed, weight_in, precision=PRECISE)
    bias_local = jnp.einsum("jkc,ch->hjk", normed, weight_bias, precision=PRECISE)
    return (projected, bias_local)


def attend(projected, bias_full, key_shift, weight_out):
    head_size = projected.shape[-1] // 4
    queries = projected[..., :head_size]
    key_proj = projected[..., head_size : 2 * head_size]
    value_proj = projected[..., 2 * head_size : 3 * head_size]
    gating = projected[..., 3 * head_size :]
    logits = jnp.einsum("ijhd,ikhd->ihjk", queries, key_proj, precision=PRECISE) * head_size ** (
        -0.5
    )
    logits = logits + bias_full[None] + key_shift
    attention = jax.nn.softmax(logits, axis=-1)
    attended = jnp.einsum("ihjk,ikhd->ijhd", attention, value_proj, precision=PRECISE)
    gated_out = jax.nn.sigmoid(gating) * attended
    return jnp.einsum("ijhd,hdc->ijc", gated_out, weight_out, precision=PRECISE)


def tri_forward(rows_in, scales, weight_in, weight_bias, weight_out, key_shift, pair_mask):

    def local_prep(values):
        return prepare(values, scales, weight_in, weight_bias)

    (projected, bias_local), pull_prep = jax.vjp(local_prep, rows_in)
    bias_full = lax.all_gather(bias_local, ("row", "head"), axis=1, tiled=True)

    def local_attend(proj_in, bias_in):
        return attend(proj_in, bias_in, key_shift, weight_out)

    partial_out, pull_attend = jax.vjp(local_attend, projected, bias_full)
    total_out = core_total(partial_out)
    return (rows_in + total_out * pair_mask, (pull_prep, pull_attend))


def tri_backward(grad_out, saved, pair_mask):
    pull_prep, pull_attend = saved
    grad_proj, grad_bias = pull_attend(grad_out * pair_mask)
    grad_local = lax.psum_scatter(grad_bias, ("row", "head"), scatter_dimension=1, tiled=True)
    (grad_rows,) = pull_prep((grad_proj, grad_local))
    return grad_out + core_total(grad_rows)


def spread_body(
    pair_acts,
    alignment,
    align_mask,
    residue_mask,
    align_gain,
    outer_in,
    outer_out,
    tri_gain,
    tri_in,
    tri_bias,
    tri_out,
    pair_cotangent,
):
    row_count = pair_acts.shape[0]
    live = residue_mask.astype(jnp.float32)
    key_shift = (live - 1.0) * MASK_SHIFT
    row_live = lax.dynamic_slice_in_dim(
        live, lax.axis_index(("row", "head")) * row_count, row_count, 0
    )
    pair_mask = row_live[:, None, None] * live[None, :, None]
    seq_count = alignment.shape[0]
    mask_all = align_mask.astype(jnp.float32)
    mask_own = lax.dynamic_slice_in_dim(mask_all, lax.axis_index("br") * seq_count, seq_count, 0)
    normed = normalize(alignment, align_gain)
    projected = jnp.einsum("snc,ck->snk", normed, outer_in, precision=PRECISE)
    left_part = projected[..., :OPC] * mask_own[..., None]
    right_part = jnp.swapaxes(projected[..., OPC:] * mask_own[..., None], 1, 2)
    right_all, mask_cols = (
        lax.all_gather(right_part, ("row", "head"), axis=2, tiled=True),
        lax.all_gather(mask_all, ("row", "head"), axis=1, tiled=True),
    )
    counts = jnp.einsum("si,sj->ij", mask_all, mask_cols, precision=PRECISE)
    table = outer_out.reshape(OPC, OPC, outer_out.shape[-1])
    mixed_left = jnp.einsum("sip,pqc->siqc", left_part, table, precision=PRECISE)
    partial_outer = jnp.einsum("siqc,sqj->ijc", mixed_left, right_all, precision=PRECISE)
    outer_sum = core_total(partial_outer)
    pair_one = pair_acts + outer_sum / counts[..., None]
    pair_two, saved_start = tri_forward(
        pair_one, tri_gain[0], tri_in[0], tri_bias[0], tri_out[0], key_shift, pair_mask
    )
    turned_two = reorient(pair_two)
    turned_three, saved_end = tri_forward(
        turned_two, tri_gain[1], tri_in[1], tri_bias[1], tri_out[1], key_shift, pair_mask
    )
    pair_out = reorient(turned_three)
    grad_turned = reorient(pair_cotangent)
    grad_turned = tri_backward(grad_turned, saved_end, pair_mask)
    grad_two = reorient(grad_turned)
    pair_grad = tri_backward(grad_two, saved_start, pair_mask)
    return (pair_out, pair_grad)


MESH_ID = pl.DeviceIdType.MESH
FUSED_BYTES = 1 << 20
NN = ((1,), (0,))
NT = ((1,), (1,))
TN = ((0,), (0,))


def split(values):
    high = values.astype(jnp.bfloat16)
    low = (values - high.astype(jnp.float32)).astype(jnp.bfloat16)
    return (high, low)


def pair_dot(first, second, dims):
    def one(a, b):
        return lax.dot_general(a, b, (dims, ((), ())), preferred_element_type=jnp.float32)

    return one(first[0], second[0]) + (one(first[0], second[1]) + one(first[1], second[0]))


def standardize(values):
    average = jnp.mean(values, axis=-1, keepdims=True)
    centred = values - average
    spread = jnp.mean(centred * centred, axis=-1, keepdims=True)
    inverse = lax.rsqrt(spread + EPSILON)
    return (centred * inverse, inverse)


def fused_kernel(
    sizes,
    live_ref,
    acts_hbm,
    align_hbm,
    mask_hbm,
    gain_hbm,
    outer_in_hbm,
    outer_out_hbm,
    tri_gain_hbm,
    tri_in_hbm,
    tri_bias_hbm,
    tri_out_hbm,
    cot_hbm,
    out_ref,
    acts_all,
    cot_all,
    proj_all,
    align_v,
    mask_v,
    gain_v,
    outer_in_v,
    outer_out_v,
    tri_gain_v,
    tri_in_all,
    tri_bias_all,
    tri_out_all,
    table_hi,
    table_lo,
    wide_hi,
    wide_lo,
    turn_v,
    mixed_v,
    load_sems,
    send_acts,
    recv_acts,
    send_proj,
    recv_proj,
    send_cot,
    recv_cot,
    send_w,
    recv_w,
):
    rows_n, heads_n, cores_n = sizes
    count = rows_n * heads_n
    chan = acts_all.shape[-1]
    my_row = lax.axis_index("row")
    my_head = lax.axis_index("head")
    my_core = lax.axis_index("br")
    me = my_row * heads_n + my_head
    seqs = align_v.shape[0]
    half = tri_in_all.shape[3]
    head_count = half * cores_n
    size = tri_in_all.shape[4] // 4
    width = head_count * size

    peers = [
        (dr, dh, db)
        for dr in range(rows_n)
        for dh in range(heads_n)
        for db in range(cores_n)
        if (dr, dh, db) != (0, 0, 0)
    ]

    def place(offset):
        dr, dh, db = offset
        return (
            lax.rem(my_row + dr, rows_n),
            lax.rem(my_head + dh, heads_n),
            lax.rem(my_core + db, cores_n),
        )

    def target(offset):
        row, head, core = place(offset)
        return {"row": row, "head": head, "br": core}

    barrier = pltpu.get_barrier_semaphore()
    for offset in peers:
        pl.semaphore_signal(barrier, inc=1, device_id=target(offset), device_id_type=MESH_ID)

    loads = [
        pltpu.make_async_copy(align_hbm, align_v, load_sems.at[0]),
        pltpu.make_async_copy(gain_hbm, gain_v, load_sems.at[1]),
        pltpu.make_async_copy(outer_in_hbm, outer_in_v, load_sems.at[2]),
        pltpu.make_async_copy(mask_hbm, mask_v, load_sems.at[3]),
        pltpu.make_async_copy(acts_hbm.at[0], acts_all.at[me, 0:count], load_sems.at[4]),
        pltpu.make_async_copy(tri_in_hbm, tri_in_all.at[my_core], load_sems.at[5]),
        pltpu.make_async_copy(tri_bias_hbm, tri_bias_all.at[my_core], load_sems.at[6]),
        pltpu.make_async_copy(tri_out_hbm, tri_out_all.at[my_core], load_sems.at[7]),
        pltpu.make_async_copy(cot_hbm.at[0], cot_all.at[me], load_sems.at[8]),
        pltpu.make_async_copy(outer_out_hbm, outer_out_v, load_sems.at[9]),
        pltpu.make_async_copy(tri_gain_hbm, tri_gain_v, load_sems.at[10]),
    ]
    for load in loads:
        load.start()
    for load in loads[:4]:
        load.wait()

    aligned = align_v[:, 0, :]
    normed = standardize(aligned)[0] * gain_v[...]
    projected = pair_dot(split(normed), split(outer_in_v[...]), NT)
    mask_f = mask_v[...].astype(jnp.float32)
    depth = mask_f.shape[1]
    lane = lax.broadcasted_iota(jnp.int32, (seqs, depth), 1)
    own_s = lax.broadcasted_iota(jnp.int32, (seqs, depth), 0) + my_core * seqs
    mask_own = jnp.sum(jnp.where(lane == own_s, mask_f, 0.0), axis=1, keepdims=True)
    projected = projected * mask_own
    pieces = seqs // 8
    proj_all[my_core, me] = jnp.concatenate(
        [projected[8 * piece : 8 * piece + 8] for piece in range(pieces)], axis=1
    )
    acts_all[me, count : count + 1] = jnp.concatenate(
        [mask_f, jnp.zeros((1, chan - depth), jnp.float32)], axis=1
    )
    for load in loads[4:]:
        load.wait()

    pl.semaphore_wait(barrier, len(peers))

    sends = []
    receives = []
    weight_receives = []
    cot_receives = []

    def remote(src, dst, send_sem, recv_sem, offset):
        return pltpu.make_async_remote_copy(
            src_ref=src,
            dst_ref=dst,
            send_sem=send_sem,
            recv_sem=recv_sem,
            device_id=target(offset),
            device_id_type=MESH_ID,
        )

    ordered = sorted(peers, key=lambda o: -(min(o[0], rows_n - o[0]) + o[1]))
    for number, offset in enumerate(ordered):
        row, head, core = place(offset)
        other = row * heads_n + head
        copy = remote(
            proj_all.at[my_core, me],
            proj_all.at[my_core, me],
            send_proj.at[number],
            recv_proj.at[my_core, me],
            offset,
        )
        copy.start()
        sends.append(copy)
        receives.append(
            remote(
                proj_all.at[core, other],
                proj_all.at[core, other],
                send_proj.at[number],
                recv_proj.at[core, other],
                offset,
            )
        )
        if offset[2] == 0:
            copy = remote(
                acts_all.at[me, 0 : count + 1],
                acts_all.at[me, 0 : count + 1],
                send_acts.at[number],
                recv_acts.at[me],
                offset,
            )
            copy.start()
            sends.append(copy)
            receives.append(
                remote(
                    acts_all.at[other, 0 : count + 1],
                    acts_all.at[other, 0 : count + 1],
                    send_acts.at[number],
                    recv_acts.at[other],
                    offset,
                )
            )
    for db in range(1, cores_n):
        offset = (0, 0, db)
        core = lax.rem(my_core + db, cores_n)
        for which, ref in enumerate((tri_in_all, tri_bias_all, tri_out_all)):
            copy = remote(
                ref.at[my_core],
                ref.at[my_core],
                send_w.at[which, db],
                recv_w.at[which, my_core],
                offset,
            )
            copy.start()
            sends.append(copy)
            weight_receives.append(
                remote(
                    ref.at[core],
                    ref.at[core],
                    send_w.at[which, db],
                    recv_w.at[which, core],
                    offset,
                )
            )
    for number, offset in enumerate(ordered):
        if offset[2] == 0:
            row, head, core = place(offset)
            other = row * heads_n + head
            copy = remote(
                cot_all.at[me], cot_all.at[me], send_cot.at[number], recv_cot.at[me], offset
            )
            copy.start()
            sends.append(copy)
            cot_receives.append(
                remote(
                    cot_all.at[other],
                    cot_all.at[other],
                    send_cot.at[number],
                    recv_cot.at[other],
                    offset,
                )
            )

    for q in range(OPC):
        high, low = split(outer_out_v[pl.ds(q, OPC, stride=OPC), :])
        table_hi[q * OPC : (q + 1) * OPC] = high
        table_lo[q * OPC : (q + 1) * OPC] = low

    pairs = count * count
    lanes = head_count * pairs
    tile_row = lax.broadcasted_iota(jnp.int32, (count, count, lanes), 0)
    lane_at = lax.rem(lax.broadcasted_iota(jnp.int32, (count, count, lanes), 2), pairs)
    at_first = tile_row == lane_at // count
    at_second = tile_row == lax.rem(lane_at, count)
    live = [live_ref[n].astype(jnp.float32) for n in range(count)]
    key_at = lax.broadcasted_iota(jnp.int32, (count, lanes), 0)
    first_at = lax.broadcasted_iota(jnp.int32, (count, count, chan), 0)
    second_at = lax.broadcasted_iota(jnp.int32, (count, count, chan), 1)
    key_live = jnp.zeros((count, lanes), jnp.float32)
    live_first = jnp.zeros((count, count, chan), jnp.float32)
    live_second = jnp.zeros((count, count, chan), jnp.float32)
    for n in range(count):
        key_live = jnp.where(key_at == n, live[n], key_live)
        live_first = jnp.where(first_at == n, live[n], live_first)
        live_second = jnp.where(second_at == n, live[n], live_second)
    key_shift = (key_live - 1.0) * MASK_SHIFT
    pair_mask = (live_first * live_second).reshape(pairs, chan)
    lane_head = lax.broadcasted_iota(jnp.int32, (pairs, width), 1) // size

    def heads_apart(values):
        return jnp.concatenate(
            [jnp.where(lane_head == h, values, 0.0) for h in range(head_count)], axis=0
        )

    def heads_together(values):
        total = jnp.where(lane_head == 0, values[0:pairs], 0.0)
        for h in range(1, head_count):
            total = jnp.where(lane_head == h, values[h * pairs : (h + 1) * pairs], total)
        return total

    def spread_over(values, where):
        return jnp.where(where, values[None], 0.0).reshape(pairs, lanes)

    def fold(values, where):
        return jnp.sum(jnp.where(where, values.reshape(count, count, lanes), 0.0), axis=0)

    for receive in weight_receives:
        receive.wait_recv()

    outs = []
    for t in range(2):
        blocks = []
        for h in range(head_count):
            blocks.append(tri_in_all[h // half, t, :, h % half, :])
        for block in range(4):
            columns = jnp.concatenate(
                [b[:, block * size : (block + 1) * size] for b in blocks], axis=1
            )
            high, low = split(columns)
            wide_hi[t, :, block * width : (block + 1) * width] = high
            wide_lo[t, :, block * width : (block + 1) * width] = low
        bias_rows = jnp.concatenate(
            [tri_bias_all[core, t] for core in range(cores_n)]
            + [jnp.zeros((chan - head_count, chan), jnp.float32)],
            axis=0,
        )
        bias_turned = bias_rows.T
        bias_columns = jnp.concatenate(
            [
                jnp.broadcast_to(bias_turned[:, h : h + 1], (chan, pairs))
                for h in range(head_count)
            ],
            axis=1,
        )
        high, low = split(bias_columns)
        wide_hi[t, :, 4 * width :] = high
        wide_lo[t, :, 4 * width :] = low
        outs.append(
            split(
                jnp.concatenate(
                    [tri_out_all[h // half, t, h % half] for h in range(head_count)], axis=0
                )
            )
        )

    for receive in receives:
        receive.wait_recv()

    left_tiles = []
    right_tiles = []
    for core in range(cores_n):
        for piece in range(pieces):
            base = piece * 2 * OPC
            left_tiles.append(
                jnp.concatenate(
                    [proj_all[core, n, :, base : base + OPC] for n in range(count)], axis=1
                )
            )
            right_tiles.append(
                jnp.concatenate(
                    [proj_all[core, n, :, base + OPC : base + 2 * OPC] for n in range(count)],
                    axis=1,
                )
            )
    left = jnp.concatenate(left_tiles, axis=0)
    right = jnp.concatenate(right_tiles, axis=0)
    mixed = pair_dot(split(right), split(left), TN)
    for block in range(mixed_v.shape[0]):
        mixed_v[block] = mixed[:, block * chan : (block + 1) * chan]
    strips = [[] for _ in range(count)]
    for q in range(OPC):
        for block in range(mixed_v.shape[0]):
            tile = mixed_v[block, pl.ds(q, count, stride=OPC), :]
            for n in range(chan // OPC):
                strips[block * (chan // OPC) + n].append(tile[:, n * OPC : (n + 1) * OPC])
    crossed = jnp.concatenate([jnp.concatenate(s, axis=1) for s in strips], axis=0)
    summed = pair_dot(split(crossed), (table_hi[...], table_lo[...]), NN)
    mask_rows = jnp.concatenate([acts_all[n, count : count + 1] for n in range(count)], axis=0)
    counts = jnp.sum(mask_rows[:, None, :] * mask_rows[None, :, :], axis=-1, keepdims=True)
    acts = jnp.concatenate([acts_all[n, 0:count] for n in range(count)], axis=0)
    pair_one = acts + summed / counts.reshape(pairs, 1)

    def turn(values):
        turn_v[...] = values
        return jnp.concatenate(
            [turn_v[pl.ds(n, count, stride=count), :] for n in range(count)], axis=0
        )

    scale = size ** (-0.5)

    def forward(x, t):
        gain = tri_gain_v[t : t + 1]
        hat, inverse = standardize(x)
        weights = (wide_hi[t], wide_lo[t])
        projected = pair_dot(split(hat * gain), weights, NN)
        query = projected[:, 0:width] * scale
        key = split(projected[:, width : 2 * width])
        value = split(projected[:, 2 * width : 3 * width])
        gate = jax.nn.sigmoid(projected[:, 3 * width : 4 * width])
        bias = fold(projected[:, 4 * width :], at_second)
        query_apart = split(heads_apart(query))
        logits = fold(pair_dot(key, query_apart, NT), at_first) + bias + key_shift
        top = jnp.max(logits, axis=0, keepdims=True)
        exps = jnp.exp(logits - top)
        probs = exps / jnp.sum(exps, axis=0, keepdims=True)
        probs_wide = split(spread_over(probs, at_first))
        attended = heads_together(pair_dot(probs_wide, value, TN))
        update = pair_dot(split(gate * attended), outs[t], NN)
        saved = (hat, inverse, gain, weights, key, value, gate, query_apart, probs, probs_wide, attended)
        return (x + update * pair_mask, saved)

    def backward(grad, t, saved):
        hat, inverse, gain, weights, key, value, gate, query_apart, probs, probs_wide, attended = saved
        d_gated = pair_dot(split(grad * pair_mask), outs[t], NT)
        d_gate = d_gated * attended * gate * (1.0 - gate)
        d_apart = split(heads_apart(d_gated * gate))
        d_probs = fold(pair_dot(value, d_apart, NT), at_first)
        d_value = pair_dot(probs_wide, d_apart, NN)
        d_logits = probs * (d_probs - jnp.sum(probs * d_probs, axis=0, keepdims=True))
        d_wide = split(spread_over(d_logits, at_first))
        d_key = pair_dot(d_wide, query_apart, NN)
        d_query = heads_together(pair_dot(d_wide, key, TN)) * scale
        d_bias = spread_over(d_logits, at_second)
        d_all = jnp.concatenate([d_query, d_key, d_value, d_gate, d_bias], axis=1)
        d_normed = pair_dot(split(d_all), weights, NT) * gain
        mean_d = jnp.mean(d_normed, axis=-1, keepdims=True)
        mean_dh = jnp.mean(d_normed * hat, axis=-1, keepdims=True)
        return grad + inverse * (d_normed - mean_d - hat * mean_dh)

    pair_two, saved_start = forward(pair_one, 0)
    turned, saved_end = forward(turn(pair_two), 1)
    turn_v[...] = turned
    out_ref[0] = turn_v[pl.ds(me, count, stride=count), :]

    for receive in cot_receives:
        receive.wait_recv()
    cot = jnp.concatenate(
        [cot_all[:, n, :] for n in range(count)], axis=0
    )
    grad_two = turn(backward(cot, 1, saved_end))
    turn_v[...] = backward(grad_two, 0, saved_start)
    out_ref[1] = turn_v[pl.ds(pl.multiple_of(me * count, count), count), :]

    for copy in sends:
        copy.wait_send()


def fused_body(shape, args):
    (
        pair_acts,
        alignment,
        align_mask,
        residue_mask,
        align_gain,
        outer_in,
        outer_out,
        tri_gain,
        tri_in,
        tri_bias,
        tri_out,
        pair_cotangent,
    ) = args
    rows_n, heads_n, cores_n = shape["row"], shape["head"], shape["br"]
    count = rows_n * heads_n
    chan = pair_acts.shape[-1]
    seqs = alignment.shape[0]
    half, size = tri_in.shape[2], tri_in.shape[3] // 4
    head_count = half * cores_n
    lanes = head_count * count * count
    wide = 4 * head_count * size + lanes
    others = count * cores_n
    f32, b16 = jnp.float32, jnp.bfloat16
    anywhere = pl.BlockSpec(memory_space=pl.ANY)
    here = pl.BlockSpec(memory_space=pltpu.VMEM)
    dma = pltpu.SemaphoreType.DMA
    scratch = [
        pltpu.VMEM((count, count + 8, chan), f32),
        pltpu.VMEM((count, count, chan), f32),
        pltpu.VMEM((cores_n, count, 8, (seqs // 8) * 2 * OPC), f32),
        pltpu.VMEM(alignment.shape, f32),
        pltpu.VMEM(align_mask.shape[::-1], jnp.int32),
        pltpu.VMEM((1, align_gain.shape[0]), f32),
        pltpu.VMEM(outer_in.shape[::-1], f32),
        pltpu.VMEM(outer_out.shape, f32),
        pltpu.VMEM(tri_gain.shape, f32),
        pltpu.VMEM((cores_n,) + tri_in.shape, f32),
        pltpu.VMEM((cores_n, 2, half, chan), f32),
        pltpu.VMEM((cores_n,) + tri_out.shape, f32),
        pltpu.VMEM(outer_out.shape, b16),
        pltpu.VMEM(outer_out.shape, b16),
        pltpu.VMEM((2, chan, wide), b16),
        pltpu.VMEM((2, chan, wide), b16),
        pltpu.VMEM((count * count, chan), f32),
        pltpu.VMEM((count * OPC // chan, count * OPC, chan), f32),
        dma((11,)),
        dma((others,)),
        dma((count,)),
        dma((others,)),
        dma((cores_n, count)),
        dma((others,)),
        dma((count,)),
        dma((3, cores_n)),
        dma((3, cores_n)),
    ]
    both = pl.pallas_call(
        functools.partial(fused_kernel, (rows_n, heads_n, cores_n)),
        out_shape=jax.ShapeDtypeStruct((2,) + pair_acts.shape[1:], f32),
        in_specs=[pl.BlockSpec(memory_space=pltpu.SMEM)] + [anywhere] * 11,
        out_specs=here,
        scratch_shapes=scratch,
        compiler_params=pltpu.CompilerParams(collective_id=0, has_side_effects=True),
    )(
        residue_mask,
        pair_acts,
        alignment,
        align_mask.T,
        align_gain[None],
        outer_in.T,
        outer_out,
        tri_gain,
        tri_in,
        jnp.swapaxes(tri_bias, 1, 2),
        tri_out,
        pair_cotangent,
    )
    return (both[0:1], both[1:2])


def dispatch(shape, *args):
    pair_acts, alignment, align_mask, tri_in = args[0], args[1], args[2], args[8]
    count = pair_acts.shape[1]
    head_count = tri_in.shape[2] * shape["br"]
    chan = pair_acts.shape[-1]
    fits = (
        pair_acts.shape[0] == 1
        and alignment.shape[1] == 1
        and count % 8 == 0
        and alignment.shape[0] % 8 == 0
        and align_mask.shape[0] <= chan
        and head_count * (tri_in.shape[3] // 4) == chan
        and head_count * count**4 * 4 <= FUSED_BYTES
    )
    return fused_body(shape, args) if fits else spread_body(*args)


def solution(mesh):
    in_specs = (
        P(("grp", "row", "head"), None, None),
        P(("grp", "br"), ("row", "head"), None),
        P("grp", ("row", "head")),
        P("grp"),
        P(),
        P(),
        P(),
        P(),
        P(None, None, "br", None),
        P(None, None, "br"),
        P(None, "br", None, None),
        P(("grp", "row", "head"), None, None),
    )
    out_specs = (P(("grp", "row", "head"), None, None), P(("grp", "row", "head"), None, None))
    return jax.shard_map(functools.partial(dispatch, dict(mesh.shape)), mesh=mesh, in_specs=in_specs, out_specs=out_specs, check_vma=False)
```

```python
import functools

import jax
import jax.numpy as jnp
from jax import lax
from jax.experimental import pallas as pl
from jax.experimental.pallas import tpu as pltpu
from jax.sharding import PartitionSpec as P

OPC = 32


PRECISE = lax.Precision.HIGHEST
EPSILON = 1e-05
MASK_SHIFT = 1000000000.0


def normalize(values, scales):
    average = jnp.mean(values, axis=-1, keepdims=True)
    centred = values - average
    spread = jnp.mean(centred * centred, axis=-1, keepdims=True)
    return centred * lax.rsqrt(spread + EPSILON) * scales


def core_total(values):
    return lax.psum(values, "br")


def reorient(values):
    turned = jnp.swapaxes(values, 0, 1)
    return lax.all_to_all(turned, ("row", "head"), split_axis=0, concat_axis=1, tiled=True)


def prepare(values, scales, weight_in, weight_bias):
    normed = normalize(values, scales)
    projected = jnp.einsum("ijc,chd->ijhd", normed, weight_in, precision=PRECISE)
    bias_local = jnp.einsum("jkc,ch->hjk", normed, weight_bias, precision=PRECISE)
    return (projected, bias_local)


def attend(projected, bias_full, key_shift, weight_out):
    head_size = projected.shape[-1] // 4
    queries = projected[..., :head_size]
    key_proj = projected[..., head_size : 2 * head_size]
    value_proj = projected[..., 2 * head_size : 3 * head_size]
    gating = projected[..., 3 * head_size :]
    logits = jnp.einsum("ijhd,ikhd->ihjk", queries, key_proj, precision=PRECISE) * head_size ** (
        -0.5
    )
    logits = logits + bias_full[None] + key_shift
    attention = jax.nn.softmax(logits, axis=-1)
    attended = jnp.einsum("ihjk,ikhd->ijhd", attention, value_proj, precision=PRECISE)
    gated_out = jax.nn.sigmoid(gating) * attended
    return jnp.einsum("ijhd,hdc->ijc", gated_out, weight_out, precision=PRECISE)


def tri_forward(rows_in, scales, weight_in, weight_bias, weight_out, key_shift, pair_mask):

    def local_prep(values):
        return prepare(values, scales, weight_in, weight_bias)

    (projected, bias_local), pull_prep = jax.vjp(local_prep, rows_in)
    bias_full = lax.all_gather(bias_local, ("row", "head"), axis=1, tiled=True)

    def local_attend(proj_in, bias_in):
        return attend(proj_in, bias_in, key_shift, weight_out)

    partial_out, pull_attend = jax.vjp(local_attend, projected, bias_full)
    total_out = core_total(partial_out)
    return (rows_in + total_out * pair_mask, (pull_prep, pull_attend))


def tri_backward(grad_out, saved, pair_mask):
    pull_prep, pull_attend = saved
    grad_proj, grad_bias = pull_attend(grad_out * pair_mask)
    grad_local = lax.psum_scatter(grad_bias, ("row", "head"), scatter_dimension=1, tiled=True)
    (grad_rows,) = pull_prep((grad_proj, grad_local))
    return grad_out + core_total(grad_rows)


def spread_body(
    pair_acts,
    alignment,
    align_mask,
    residue_mask,
    align_gain,
    outer_in,
    outer_out,
    tri_gain,
    tri_in,
    tri_bias,
    tri_out,
    pair_cotangent,
):
    row_count = pair_acts.shape[0]
    live = residue_mask.astype(jnp.float32)
    key_shift = (live - 1.0) * MASK_SHIFT
    row_live = lax.dynamic_slice_in_dim(
        live, lax.axis_index(("row", "head")) * row_count, row_count, 0
    )
    pair_mask = row_live[:, None, None] * live[None, :, None]
    seq_count = alignment.shape[0]
    mask_all = align_mask.astype(jnp.float32)
    mask_own = lax.dynamic_slice_in_dim(mask_all, lax.axis_index("br") * seq_count, seq_count, 0)
    normed = normalize(alignment, align_gain)
    projected = jnp.einsum("snc,ck->snk", normed, outer_in, precision=PRECISE)
    left_part = projected[..., :OPC] * mask_own[..., None]
    right_part = jnp.swapaxes(projected[..., OPC:] * mask_own[..., None], 1, 2)
    right_all, mask_cols = (
        lax.all_gather(right_part, ("row", "head"), axis=2, tiled=True),
        lax.all_gather(mask_all, ("row", "head"), axis=1, tiled=True),
    )
    counts = jnp.einsum("si,sj->ij", mask_all, mask_cols, precision=PRECISE)
    table = outer_out.reshape(OPC, OPC, outer_out.shape[-1])
    mixed_left = jnp.einsum("sip,pqc->siqc", left_part, table, precision=PRECISE)
    partial_outer = jnp.einsum("siqc,sqj->ijc", mixed_left, right_all, precision=PRECISE)
    outer_sum = core_total(partial_outer)
    pair_one = pair_acts + outer_sum / counts[..., None]
    pair_two, saved_start = tri_forward(
        pair_one, tri_gain[0], tri_in[0], tri_bias[0], tri_out[0], key_shift, pair_mask
    )
    turned_two = reorient(pair_two)
    turned_three, saved_end = tri_forward(
        turned_two, tri_gain[1], tri_in[1], tri_bias[1], tri_out[1], key_shift, pair_mask
    )
    pair_out = reorient(turned_three)
    grad_turned = reorient(pair_cotangent)
    grad_turned = tri_backward(grad_turned, saved_end, pair_mask)
    grad_two = reorient(grad_turned)
    pair_grad = tri_backward(grad_two, saved_start, pair_mask)
    return (pair_out, pair_grad)


MESH_ID = pl.DeviceIdType.MESH
FUSED_BYTES = 1 << 20
NN = ((1,), (0,))
NT = ((1,), (1,))
TN = ((0,), (0,))


def split(values):
    high = values.astype(jnp.bfloat16)
    low = (values - high.astype(jnp.float32)).astype(jnp.bfloat16)
    return (high, low)


def pair_dot(first, second, dims):
    def one(a, b):
        return lax.dot_general(a, b, (dims, ((), ())), preferred_element_type=jnp.float32)

    a = jnp.concatenate([first[0], first[1], first[0]], axis=dims[0][0])
    b = jnp.concatenate([second[0], second[0], second[1]], axis=dims[1][0])
    return one(a, b)


def standardize(values):
    average = jnp.mean(values, axis=-1, keepdims=True)
    centred = values - average
    spread = jnp.mean(centred * centred, axis=-1, keepdims=True)
    inverse = lax.rsqrt(spread + EPSILON)
    return (centred * inverse, inverse)


def fused_kernel(
    sizes,
    live_ref,
    acts_hbm,
    align_hbm,
    mask_hbm,
    gain_hbm,
    outer_in_hbm,
    outer_out_hbm,
    tri_gain_hbm,
    tri_in_hbm,
    tri_bias_hbm,
    tri_out_hbm,
    cot_hbm,
    out_ref,
    block_all,
    cot_all,
    align_v,
    mask_v,
    gain_v,
    outer_in_v,
    outer_out_v,
    tri_gain_v,
    tri_in_all,
    tri_bias_all,
    tri_out_all,
    table_hi,
    table_lo,
    wide_hi,
    wide_lo,
    turn_v,
    mixed_v,
    load_sems,
    send_block,
    recv_block,
    send_cot,
    recv_cot,
    send_w,
    recv_w,
):
    rows_n, heads_n, cores_n = sizes
    count = rows_n * heads_n
    chan = cot_all.shape[-1]
    my_row = lax.axis_index("row")
    my_head = lax.axis_index("head")
    my_core = lax.axis_index("br")
    me = my_row * heads_n + my_head
    seqs = align_v.shape[0]
    half = tri_in_all.shape[3]
    head_count = half * cores_n
    size = tri_in_all.shape[4] // 4
    width = head_count * size

    peers = [
        (dr, dh, db)
        for dr in range(rows_n)
        for dh in range(heads_n)
        for db in range(cores_n)
        if (dr, dh, db) != (0, 0, 0)
    ]

    def place(offset):
        dr, dh, db = offset
        return (
            lax.rem(my_row + dr, rows_n),
            lax.rem(my_head + dh, heads_n),
            lax.rem(my_core + db, cores_n),
        )

    def target(offset):
        row, head, core = place(offset)
        return {"row": row, "head": head, "br": core}

    barrier = pltpu.get_barrier_semaphore()
    for offset in peers:
        pl.semaphore_signal(barrier, inc=1, device_id=target(offset), device_id_type=MESH_ID)

    loads = [
        pltpu.make_async_copy(align_hbm, align_v, load_sems.at[0]),
        pltpu.make_async_copy(gain_hbm, gain_v, load_sems.at[1]),
        pltpu.make_async_copy(outer_in_hbm, outer_in_v, load_sems.at[2]),
        pltpu.make_async_copy(mask_hbm, mask_v, load_sems.at[3]),
        pltpu.make_async_copy(acts_hbm.at[0], block_all.at[my_core, me, 0:count], load_sems.at[4]),
        pltpu.make_async_copy(tri_in_hbm, tri_in_all.at[my_core], load_sems.at[5]),
        pltpu.make_async_copy(tri_bias_hbm, tri_bias_all.at[my_core], load_sems.at[6]),
        pltpu.make_async_copy(tri_out_hbm, tri_out_all.at[my_core], load_sems.at[7]),
        pltpu.make_async_copy(cot_hbm.at[0], cot_all.at[me], load_sems.at[8]),
        pltpu.make_async_copy(outer_out_hbm, outer_out_v, load_sems.at[9]),
        pltpu.make_async_copy(tri_gain_hbm, tri_gain_v, load_sems.at[10]),
    ]
    for load in loads:
        load.start()
    for load in loads[:4]:
        load.wait()

    aligned = align_v[:, 0, :]
    normed = standardize(aligned)[0] * gain_v[...]
    projected = pair_dot(split(normed), split(outer_in_v[...]), NT)
    mask_f = mask_v[...].astype(jnp.float32)
    depth = mask_f.shape[1]
    lane = lax.broadcasted_iota(jnp.int32, (seqs, depth), 1)
    own_s = lax.broadcasted_iota(jnp.int32, (seqs, depth), 0) + my_core * seqs
    mask_own = jnp.sum(jnp.where(lane == own_s, mask_f, 0.0), axis=1, keepdims=True)
    projected = projected * mask_own
    pieces = seqs // 8
    block_all[my_core, me, count : count + 8] = jnp.concatenate(
        [projected[8 * piece : 8 * piece + 8] for piece in range(pieces)], axis=1
    )
    block_all[my_core, me, count + 8 : count + 9] = jnp.concatenate(
        [mask_f, jnp.zeros((1, chan - depth), jnp.float32)], axis=1
    )
    for load in loads[4:]:
        load.wait()

    pl.semaphore_wait(barrier, len(peers))

    sends = []
    receives = []
    weight_receives = []
    cot_receives = []

    def remote(src, dst, send_sem, recv_sem, offset):
        return pltpu.make_async_remote_copy(
            src_ref=src,
            dst_ref=dst,
            send_sem=send_sem,
            recv_sem=recv_sem,
            device_id=target(offset),
            device_id_type=MESH_ID,
        )

    ordered = sorted(peers, key=lambda o: -(min(o[0], rows_n - o[0]) + o[1]))
    for number, offset in enumerate(ordered):
        row, head, core = place(offset)
        other = row * heads_n + head
        span = slice(0, count + 9) if offset[2] == 0 else slice(count, count + 8)
        mine = block_all.at[my_core, me, span]
        theirs = block_all.at[core, other, span]
        copy = remote(mine, mine, send_block.at[number], recv_block.at[my_core, me], offset)
        copy.start()
        sends.append(copy)
        receives.append(
            remote(theirs, theirs, send_block.at[number], recv_block.at[core, other], offset)
        )
    for db in range(1, cores_n):
        offset = (0, 0, db)
        core = lax.rem(my_core + db, cores_n)
        for which, ref in enumerate((tri_in_all, tri_bias_all, tri_out_all)):
            copy = remote(
                ref.at[my_core],
                ref.at[my_core],
                send_w.at[which, db],
                recv_w.at[which, my_core],
                offset,
            )
            copy.start()
            sends.append(copy)
            weight_receives.append(
                remote(
                    ref.at[core],
                    ref.at[core],
                    send_w.at[which, db],
                    recv_w.at[which, core],
                    offset,
                )
            )
    for number, offset in enumerate(ordered):
        if offset[2] == 0:
            row, head, core = place(offset)
            other = row * heads_n + head
            copy = remote(
                cot_all.at[me], cot_all.at[me], send_cot.at[number], recv_cot.at[me], offset
            )
            copy.start()
            sends.append(copy)
            cot_receives.append(
                remote(
                    cot_all.at[other],
                    cot_all.at[other],
                    send_cot.at[number],
                    recv_cot.at[other],
                    offset,
                )
            )

    for q in range(OPC):
        high, low = split(outer_out_v[pl.ds(q, OPC, stride=OPC), :])
        table_hi[q * OPC : (q + 1) * OPC] = high
        table_lo[q * OPC : (q + 1) * OPC] = low

    pairs = count * count
    lanes = head_count * pairs
    tile_row = lax.broadcasted_iota(jnp.int32, (count, count, lanes), 0)
    lane_at = lax.rem(lax.broadcasted_iota(jnp.int32, (count, count, lanes), 2), pairs)
    at_first = tile_row == lane_at // count
    at_second = tile_row == lax.rem(lane_at, count)
    live = [live_ref[n].astype(jnp.float32) for n in range(count)]
    key_at = lax.broadcasted_iota(jnp.int32, (count, lanes), 0)
    first_at = lax.broadcasted_iota(jnp.int32, (count, count, chan), 0)
    second_at = lax.broadcasted_iota(jnp.int32, (count, count, chan), 1)
    key_live = jnp.zeros((count, lanes), jnp.float32)
    live_first = jnp.zeros((count, count, chan), jnp.float32)
    live_second = jnp.zeros((count, count, chan), jnp.float32)
    for n in range(count):
        key_live = jnp.where(key_at == n, live[n], key_live)
        live_first = jnp.where(first_at == n, live[n], live_first)
        live_second = jnp.where(second_at == n, live[n], live_second)
    key_shift = (key_live - 1.0) * MASK_SHIFT
    pair_mask = (live_first * live_second).reshape(pairs, chan)
    lane_head = lax.broadcasted_iota(jnp.int32, (pairs, width), 1) // size

    def heads_apart(values):
        return jnp.concatenate(
            [jnp.where(lane_head == h, values, 0.0) for h in range(head_count)], axis=0
        )

    def heads_together(values):
        total = jnp.where(lane_head == 0, values[0:pairs], 0.0)
        for h in range(1, head_count):
            total = jnp.where(lane_head == h, values[h * pairs : (h + 1) * pairs], total)
        return total

    def spread_over(values, where):
        return jnp.where(where, values[None], 0.0).reshape(pairs, lanes)

    def fold(values, where):
        return jnp.sum(jnp.where(where, values.reshape(count, count, lanes), 0.0), axis=0)

    for receive in weight_receives:
        receive.wait_recv()

    outs = []
    for t in range(2):
        blocks = []
        for h in range(head_count):
            blocks.append(tri_in_all[h // half, t, :, h % half, :])
        for block in range(4):
            columns = jnp.concatenate(
                [b[:, block * size : (block + 1) * size] for b in blocks], axis=1
            )
            high, low = split(columns)
            wide_hi[t, :, block * width : (block + 1) * width] = high
            wide_lo[t, :, block * width : (block + 1) * width] = low
        bias_rows = jnp.concatenate(
            [tri_bias_all[core, t] for core in range(cores_n)]
            + [jnp.zeros((chan - head_count, chan), jnp.float32)],
            axis=0,
        )
        bias_turned = bias_rows.T
        bias_columns = jnp.concatenate(
            [
                jnp.broadcast_to(bias_turned[:, h : h + 1], (chan, pairs))
                for h in range(head_count)
            ],
            axis=1,
        )
        high, low = split(bias_columns)
        wide_hi[t, :, 4 * width :] = high
        wide_lo[t, :, 4 * width :] = low
        outs.append(
            split(
                jnp.concatenate(
                    [tri_out_all[h // half, t, h % half] for h in range(head_count)], axis=0
                )
            )
        )

    for receive in receives:
        receive.wait_recv()

    left_tiles = []
    right_tiles = []
    for core in range(cores_n):
        for piece in range(pieces):
            base = piece * 2 * OPC
            left_tiles.append(
                jnp.concatenate(
                    [block_all[core, n, count : count + 8, base : base + OPC] for n in range(count)], axis=1
                )
            )
            right_tiles.append(
                jnp.concatenate(
                    [
                        block_all[core, n, count : count + 8, base + OPC : base + 2 * OPC]
                        for n in range(count)
                    ],
                    axis=1,
                )
            )
    left = jnp.concatenate(left_tiles, axis=0)
    right = jnp.concatenate(right_tiles, axis=0)
    mixed = pair_dot(split(right), split(left), TN)
    for block in range(mixed_v.shape[0]):
        mixed_v[block] = mixed[:, block * chan : (block + 1) * chan]
    strips = [[] for _ in range(count)]
    for q in range(OPC):
        for block in range(mixed_v.shape[0]):
            tile = mixed_v[block, pl.ds(q, count, stride=OPC), :]
            for n in range(chan // OPC):
                strips[block * (chan // OPC) + n].append(tile[:, n * OPC : (n + 1) * OPC])
    crossed = jnp.concatenate([jnp.concatenate(s, axis=1) for s in strips], axis=0)
    summed = pair_dot(split(crossed), (table_hi[...], table_lo[...]), NN)
    mask_rows = jnp.concatenate(
        [block_all[my_core, n, count + 8 : count + 9] for n in range(count)], axis=0
    )
    counts = jnp.sum(mask_rows[:, None, :] * mask_rows[None, :, :], axis=-1, keepdims=True)
    acts = jnp.concatenate([block_all[my_core, n, 0:count] for n in range(count)], axis=0)
    pair_one = acts + summed / counts.reshape(pairs, 1)

    def turn(values):
        turn_v[...] = values
        return jnp.concatenate(
            [turn_v[pl.ds(n, count, stride=count), :] for n in range(count)], axis=0
        )

    scale = size ** (-0.5)

    def forward(x, t):
        gain = tri_gain_v[t : t + 1]
        hat, inverse = standardize(x)
        weights = (wide_hi[t], wide_lo[t])
        projected = pair_dot(split(hat * gain), weights, NN)
        query = projected[:, 0:width] * scale
        key = split(projected[:, width : 2 * width])
        value = split(projected[:, 2 * width : 3 * width])
        gate = jax.nn.sigmoid(projected[:, 3 * width : 4 * width])
        bias = fold(projected[:, 4 * width :], at_second)
        query_apart = split(heads_apart(query))
        logits = fold(pair_dot(key, query_apart, NT), at_first) + bias + key_shift
        top = jnp.max(logits, axis=0, keepdims=True)
        exps = jnp.exp(logits - top)
        probs = exps / jnp.sum(exps, axis=0, keepdims=True)
        probs_wide = split(spread_over(probs, at_first))
        attended = heads_together(pair_dot(probs_wide, value, TN))
        update = pair_dot(split(gate * attended), outs[t], NN)
        saved = (hat, inverse, gain, weights, key, value, gate, query_apart, probs, probs_wide, attended)
        return (x + update * pair_mask, saved)

    def backward(grad, t, saved):
        hat, inverse, gain, weights, key, value, gate, query_apart, probs, probs_wide, attended = saved
        d_gated = pair_dot(split(grad * pair_mask), outs[t], NT)
        d_gate = d_gated * attended * gate * (1.0 - gate)
        d_apart = split(heads_apart(d_gated * gate))
        d_probs = fold(pair_dot(value, d_apart, NT), at_first)
        d_value = pair_dot(probs_wide, d_apart, NN)
        d_logits = probs * (d_probs - jnp.sum(probs * d_probs, axis=0, keepdims=True))
        d_wide = split(spread_over(d_logits, at_first))
        d_key = pair_dot(d_wide, query_apart, NN)
        d_query = heads_together(pair_dot(d_wide, key, TN)) * scale
        d_bias = spread_over(d_logits, at_second)
        d_all = jnp.concatenate([d_query, d_key, d_value, d_gate, d_bias], axis=1)
        d_normed = pair_dot(split(d_all), weights, NT) * gain
        mean_d = jnp.mean(d_normed, axis=-1, keepdims=True)
        mean_dh = jnp.mean(d_normed * hat, axis=-1, keepdims=True)
        return grad + inverse * (d_normed - mean_d - hat * mean_dh)

    pair_two, saved_start = forward(pair_one, 0)
    turned, saved_end = forward(turn(pair_two), 1)
    turn_v[...] = turned
    out_ref[0] = turn_v[pl.ds(me, count, stride=count), :]

    for receive in cot_receives:
        receive.wait_recv()
    cot = jnp.concatenate(
        [cot_all[:, n, :] for n in range(count)], axis=0
    )
    grad_two = turn(backward(cot, 1, saved_end))
    turn_v[...] = backward(grad_two, 0, saved_start)
    out_ref[1] = turn_v[pl.ds(pl.multiple_of(me * count, count), count), :]

    for copy in sends:
        copy.wait_send()


def fused_body(shape, args):
    (
        pair_acts,
        alignment,
        align_mask,
        residue_mask,
        align_gain,
        outer_in,
        outer_out,
        tri_gain,
        tri_in,
        tri_bias,
        tri_out,
        pair_cotangent,
    ) = args
    rows_n, heads_n, cores_n = shape["row"], shape["head"], shape["br"]
    count = rows_n * heads_n
    chan = pair_acts.shape[-1]
    seqs = alignment.shape[0]
    half, size = tri_in.shape[2], tri_in.shape[3] // 4
    head_count = half * cores_n
    lanes = head_count * count * count
    wide = 4 * head_count * size + lanes
    others = count * cores_n
    f32, b16 = jnp.float32, jnp.bfloat16
    anywhere = pl.BlockSpec(memory_space=pl.ANY)
    here = pl.BlockSpec(memory_space=pltpu.VMEM)
    dma = pltpu.SemaphoreType.DMA
    scratch = [
        pltpu.VMEM((cores_n, count, count + 16, chan), f32),
        pltpu.VMEM((count, count, chan), f32),
        pltpu.VMEM(alignment.shape, f32),
        pltpu.VMEM(align_mask.shape[::-1], jnp.int32),
        pltpu.VMEM((1, align_gain.shape[0]), f32),
        pltpu.VMEM(outer_in.shape[::-1], f32),
        pltpu.VMEM(outer_out.shape, f32),
        pltpu.VMEM(tri_gain.shape, f32),
        pltpu.VMEM((cores_n,) + tri_in.shape, f32),
        pltpu.VMEM((cores_n, 2, half, chan), f32),
        pltpu.VMEM((cores_n,) + tri_out.shape, f32),
        pltpu.VMEM(outer_out.shape, b16),
        pltpu.VMEM(outer_out.shape, b16),
        pltpu.VMEM((2, chan, wide), b16),
        pltpu.VMEM((2, chan, wide), b16),
        pltpu.VMEM((count * count, chan), f32),
        pltpu.VMEM((count * OPC // chan, count * OPC, chan), f32),
        dma((11,)),
        dma((others,)),
        dma((cores_n, count)),
        dma((others,)),
        dma((count,)),
        dma((3, cores_n)),
        dma((3, cores_n)),
    ]
    both = pl.pallas_call(
        functools.partial(fused_kernel, (rows_n, heads_n, cores_n)),
        out_shape=pltpu.VMEM((2,) + pair_acts.shape[1:], f32),
        in_specs=[pl.BlockSpec(memory_space=pltpu.SMEM)] + [anywhere] * 11,
        out_specs=here,
        scratch_shapes=scratch,
        compiler_params=pltpu.CompilerParams(collective_id=0, has_side_effects=True),
    )(
        residue_mask,
        pair_acts,
        alignment,
        align_mask.T,
        align_gain[None],
        outer_in.T,
        outer_out,
        tri_gain,
        tri_in,
        jnp.swapaxes(tri_bias, 1, 2),
        tri_out,
        pair_cotangent,
    )
    return (both[0:1], both[1:2])


def dispatch(shape, *args):
    pair_acts, alignment, align_mask, tri_in = args[0], args[1], args[2], args[8]
    count = pair_acts.shape[1]
    head_count = tri_in.shape[2] * shape["br"]
    chan = pair_acts.shape[-1]
    fits = (
        pair_acts.shape[0] == 1
        and alignment.shape[1] == 1
        and count % 8 == 0
        and alignment.shape[0] // 8 * 2 * OPC == chan
        and align_mask.shape[0] <= chan
        and head_count * (tri_in.shape[3] // 4) == chan
        and head_count * count**4 * 4 <= FUSED_BYTES
    )
    return fused_body(shape, args) if fits else spread_body(*args)


def solution(mesh):
    in_specs = (
        P(("grp", "row", "head"), None, None),
        P(("grp", "br"), ("row", "head"), None),
        P("grp", ("row", "head")),
        P("grp"),
        P(),
        P(),
        P(),
        P(),
        P(None, None, "br", None),
        P(None, None, "br"),
        P(None, "br", None, None),
        P(("grp", "row", "head"), None, None),
    )
    out_specs = (P(("grp", "row", "head"), None, None), P(("grp", "row", "head"), None, None))
    return jax.shard_map(functools.partial(dispatch, dict(mesh.shape)), mesh=mesh, in_specs=in_specs, out_specs=out_specs, check_vma=False)
```

```python
import functools

import jax
import jax.numpy as jnp
from jax import lax
from jax.experimental import pallas as pl
from jax.experimental.pallas import tpu as pltpu
from jax.sharding import PartitionSpec as P

OPC = 32


PRECISE = lax.Precision.HIGHEST
EPSILON = 1e-05
MASK_SHIFT = 1000000000.0


def normalize(values, scales):
    average = jnp.mean(values, axis=-1, keepdims=True)
    centred = values - average
    spread = jnp.mean(centred * centred, axis=-1, keepdims=True)
    return centred * lax.rsqrt(spread + EPSILON) * scales


def core_total(values):
    return lax.psum(values, "br")


def reorient(values):
    turned = jnp.swapaxes(values, 0, 1)
    return lax.all_to_all(turned, ("row", "head"), split_axis=0, concat_axis=1, tiled=True)


def prepare(values, scales, weight_in, weight_bias):
    normed = normalize(values, scales)
    projected = jnp.einsum("ijc,chd->ijhd", normed, weight_in, precision=PRECISE)
    bias_local = jnp.einsum("jkc,ch->hjk", normed, weight_bias, precision=PRECISE)
    return (projected, bias_local)


def attend(projected, bias_full, key_shift, weight_out):
    head_size = projected.shape[-1] // 4
    queries = projected[..., :head_size]
    key_proj = projected[..., head_size : 2 * head_size]
    value_proj = projected[..., 2 * head_size : 3 * head_size]
    gating = projected[..., 3 * head_size :]
    logits = jnp.einsum("ijhd,ikhd->ihjk", queries, key_proj, precision=PRECISE) * head_size ** (
        -0.5
    )
    logits = logits + bias_full[None] + key_shift
    attention = jax.nn.softmax(logits, axis=-1)
    attended = jnp.einsum("ihjk,ikhd->ijhd", attention, value_proj, precision=PRECISE)
    gated_out = jax.nn.sigmoid(gating) * attended
    return jnp.einsum("ijhd,hdc->ijc", gated_out, weight_out, precision=PRECISE)


def tri_forward(rows_in, scales, weight_in, weight_bias, weight_out, key_shift, pair_mask):

    def local_prep(values):
        return prepare(values, scales, weight_in, weight_bias)

    (projected, bias_local), pull_prep = jax.vjp(local_prep, rows_in)
    bias_full = lax.all_gather(bias_local, ("row", "head"), axis=1, tiled=True)

    def local_attend(proj_in, bias_in):
        return attend(proj_in, bias_in, key_shift, weight_out)

    partial_out, pull_attend = jax.vjp(local_attend, projected, bias_full)
    total_out = core_total(partial_out)
    return (rows_in + total_out * pair_mask, (pull_prep, pull_attend))


def tri_backward(grad_out, saved, pair_mask):
    pull_prep, pull_attend = saved
    grad_proj, grad_bias = pull_attend(grad_out * pair_mask)
    grad_local = lax.psum_scatter(grad_bias, ("row", "head"), scatter_dimension=1, tiled=True)
    (grad_rows,) = pull_prep((grad_proj, grad_local))
    return grad_out + core_total(grad_rows)


def spread_body(
    pair_acts,
    alignment,
    align_mask,
    residue_mask,
    align_gain,
    outer_in,
    outer_out,
    tri_gain,
    tri_in,
    tri_bias,
    tri_out,
    pair_cotangent,
):
    row_count = pair_acts.shape[0]
    live = residue_mask.astype(jnp.float32)
    key_shift = (live - 1.0) * MASK_SHIFT
    row_live = lax.dynamic_slice_in_dim(
        live, lax.axis_index(("row", "head")) * row_count, row_count, 0
    )
    pair_mask = row_live[:, None, None] * live[None, :, None]
    seq_count = alignment.shape[0]
    mask_all = align_mask.astype(jnp.float32)
    mask_own = lax.dynamic_slice_in_dim(mask_all, lax.axis_index("br") * seq_count, seq_count, 0)
    normed = normalize(alignment, align_gain)
    projected = jnp.einsum("snc,ck->snk", normed, outer_in, precision=PRECISE)
    left_part = projected[..., :OPC] * mask_own[..., None]
    right_part = jnp.swapaxes(projected[..., OPC:] * mask_own[..., None], 1, 2)
    right_all, mask_cols = (
        lax.all_gather(right_part, ("row", "head"), axis=2, tiled=True),
        lax.all_gather(mask_all, ("row", "head"), axis=1, tiled=True),
    )
    counts = jnp.einsum("si,sj->ij", mask_all, mask_cols, precision=PRECISE)
    table = outer_out.reshape(OPC, OPC, outer_out.shape[-1])
    mixed_left = jnp.einsum("sip,pqc->siqc", left_part, table, precision=PRECISE)
    partial_outer = jnp.einsum("siqc,sqj->ijc", mixed_left, right_all, precision=PRECISE)
    outer_sum = core_total(partial_outer)
    pair_one = pair_acts + outer_sum / counts[..., None]
    pair_two, saved_start = tri_forward(
        pair_one, tri_gain[0], tri_in[0], tri_bias[0], tri_out[0], key_shift, pair_mask
    )
    turned_two = reorient(pair_two)
    turned_three, saved_end = tri_forward(
        turned_two, tri_gain[1], tri_in[1], tri_bias[1], tri_out[1], key_shift, pair_mask
    )
    pair_out = reorient(turned_three)
    grad_turned = reorient(pair_cotangent)
    grad_turned = tri_backward(grad_turned, saved_end, pair_mask)
    grad_two = reorient(grad_turned)
    pair_grad = tri_backward(grad_two, saved_start, pair_mask)
    return (pair_out, pair_grad)


MESH_ID = pl.DeviceIdType.MESH
FUSED_BYTES = 1 << 20
NN = ((1,), (0,))
NT = ((1,), (1,))
TN = ((0,), (0,))


def split(values):
    high = values.astype(jnp.bfloat16)
    low = (values - high.astype(jnp.float32)).astype(jnp.bfloat16)
    return (high, low)


def pair_dot(first, second, dims):
    def one(a, b):
        return lax.dot_general(a, b, (dims, ((), ())), preferred_element_type=jnp.float32)

    a = jnp.concatenate([first[0], first[1], first[0]], axis=dims[0][0])
    b = jnp.concatenate([second[0], second[0], second[1]], axis=dims[1][0])
    return one(a, b)


def standardize(values):
    average = jnp.mean(values, axis=-1, keepdims=True)
    centred = values - average
    spread = jnp.mean(centred * centred, axis=-1, keepdims=True)
    inverse = lax.rsqrt(spread + EPSILON)
    return (centred * inverse, inverse)


def fused_kernel(
    sizes,
    live_ref,
    acts_hbm,
    align_hbm,
    mask_hbm,
    gain_hbm,
    outer_in_hbm,
    outer_out_hbm,
    tri_gain_hbm,
    tri_in_hbm,
    tri_bias_hbm,
    tri_out_hbm,
    cot_hbm,
    out_ref,
    block_all,
    cot_all,
    align_v,
    mask_v,
    gain_v,
    outer_in_v,
    outer_out_v,
    tri_gain_v,
    tri_in_all,
    tri_bias_all,
    tri_out_all,
    table_hi,
    table_lo,
    wide_hi,
    wide_lo,
    turn_v,
    mixed_v,
    load_sems,
    send_block,
    recv_block,
    send_cot,
    recv_cot,
    send_w,
    recv_w,
):
    rows_n, heads_n, cores_n = sizes
    count = rows_n * heads_n
    chan = cot_all.shape[-1]
    my_row = lax.axis_index("row")
    my_head = lax.axis_index("head")
    my_core = lax.axis_index("br")
    me = my_row * heads_n + my_head
    seqs = align_v.shape[0]
    half = tri_in_all.shape[3]
    head_count = half * cores_n
    size = tri_in_all.shape[4] // 4
    width = head_count * size

    peers = [
        (dr, dh, db)
        for dr in range(rows_n)
        for dh in range(heads_n)
        for db in range(cores_n)
        if (dr, dh, db) != (0, 0, 0)
    ]

    def place(offset):
        dr, dh, db = offset
        return (
            lax.rem(my_row + dr, rows_n),
            lax.rem(my_head + dh, heads_n),
            lax.rem(my_core + db, cores_n),
        )

    def target(offset):
        row, head, core = place(offset)
        return {"row": row, "head": head, "br": core}

    barrier = pltpu.get_barrier_semaphore()
    for offset in peers:
        pl.semaphore_signal(barrier, inc=1, device_id=target(offset), device_id_type=MESH_ID)

    loads = [
        pltpu.make_async_copy(align_hbm, align_v, load_sems.at[0]),
        pltpu.make_async_copy(gain_hbm, gain_v, load_sems.at[1]),
        pltpu.make_async_copy(outer_in_hbm, outer_in_v, load_sems.at[2]),
        pltpu.make_async_copy(mask_hbm, mask_v, load_sems.at[3]),
        pltpu.make_async_copy(acts_hbm.at[0], block_all.at[my_core, me, 0:count], load_sems.at[4]),
        pltpu.make_async_copy(tri_in_hbm, tri_in_all.at[my_core], load_sems.at[5]),
        pltpu.make_async_copy(tri_bias_hbm, tri_bias_all.at[my_core], load_sems.at[6]),
        pltpu.make_async_copy(tri_out_hbm, tri_out_all.at[my_core], load_sems.at[7]),
        pltpu.make_async_copy(cot_hbm.at[0], cot_all.at[me], load_sems.at[8]),
        pltpu.make_async_copy(outer_out_hbm, outer_out_v, load_sems.at[9]),
        pltpu.make_async_copy(tri_gain_hbm, tri_gain_v, load_sems.at[10]),
    ]
    for load in loads:
        load.start()
    for load in loads[:4]:
        load.wait()

    aligned = align_v[:, 0, :]
    normed = standardize(aligned)[0] * gain_v[...]
    projected = pair_dot(split(normed), split(outer_in_v[...]), NT)
    mask_f = mask_v[...].astype(jnp.float32)
    depth = mask_f.shape[1]
    lane = lax.broadcasted_iota(jnp.int32, (seqs, depth), 1)
    own_s = lax.broadcasted_iota(jnp.int32, (seqs, depth), 0) + my_core * seqs
    mask_own = jnp.sum(jnp.where(lane == own_s, mask_f, 0.0), axis=1, keepdims=True)
    projected = projected * mask_own
    pieces = seqs // 8
    block_all[my_core, me, count : count + 8] = jnp.concatenate(
        [projected[8 * piece : 8 * piece + 8] for piece in range(pieces)], axis=1
    )
    block_all[my_core, me, count + 8 : count + 9] = jnp.concatenate(
        [mask_f, jnp.zeros((1, chan - depth), jnp.float32)], axis=1
    )
    for load in loads[4:]:
        load.wait()

    pl.semaphore_wait(barrier, len(peers))

    sends = []
    receives = []
    weight_receives = []
    cot_receives = []

    def remote(src, dst, send_sem, recv_sem, offset):
        return pltpu.make_async_remote_copy(
            src_ref=src,
            dst_ref=dst,
            send_sem=send_sem,
            recv_sem=recv_sem,
            device_id=target(offset),
            device_id_type=MESH_ID,
        )

    ordered = sorted(peers, key=lambda o: -(min(o[0], rows_n - o[0]) + o[1]))
    for number, offset in enumerate(ordered):
        row, head, core = place(offset)
        other = row * heads_n + head
        span = slice(0, count + 9) if offset[2] == 0 else slice(count, count + 8)
        mine = block_all.at[my_core, me, span]
        theirs = block_all.at[core, other, span]
        copy = remote(mine, mine, send_block.at[number], recv_block.at[my_core, me], offset)
        copy.start()
        sends.append(copy)
        receives.append(
            remote(theirs, theirs, send_block.at[number], recv_block.at[core, other], offset)
        )
    for db in range(1, cores_n):
        offset = (0, 0, db)
        core = lax.rem(my_core + db, cores_n)
        for which, ref in enumerate((tri_in_all, tri_bias_all, tri_out_all)):
            copy = remote(
                ref.at[my_core],
                ref.at[my_core],
                send_w.at[which, db],
                recv_w.at[which, my_core],
                offset,
            )
            copy.start()
            sends.append(copy)
            weight_receives.append(
                remote(
                    ref.at[core],
                    ref.at[core],
                    send_w.at[which, db],
                    recv_w.at[which, core],
                    offset,
                )
            )
    for number, offset in enumerate(ordered):
        if offset[2] == 0:
            row, head, core = place(offset)
            other = row * heads_n + head
            copy = remote(
                cot_all.at[me], cot_all.at[me], send_cot.at[number], recv_cot.at[me], offset
            )
            copy.start()
            sends.append(copy)
            cot_receives.append(
                remote(
                    cot_all.at[other],
                    cot_all.at[other],
                    send_cot.at[number],
                    recv_cot.at[other],
                    offset,
                )
            )

    for q in range(OPC):
        high, low = split(outer_out_v[pl.ds(q, OPC, stride=OPC), :])
        table_hi[q * OPC : (q + 1) * OPC] = high
        table_lo[q * OPC : (q + 1) * OPC] = low

    pairs = count * count
    lanes = head_count * pairs
    tile_row = lax.broadcasted_iota(jnp.int32, (count, count, lanes), 0)
    lane_at = lax.rem(lax.broadcasted_iota(jnp.int32, (count, count, lanes), 2), pairs)
    at_first = tile_row == lane_at // count
    at_second = tile_row == lax.rem(lane_at, count)
    live = [live_ref[n].astype(jnp.float32) for n in range(count)]
    key_at = lax.broadcasted_iota(jnp.int32, (count, lanes), 0)
    first_at = lax.broadcasted_iota(jnp.int32, (count, count, chan), 0)
    second_at = lax.broadcasted_iota(jnp.int32, (count, count, chan), 1)
    key_live = jnp.zeros((count, lanes), jnp.float32)
    live_first = jnp.zeros((count, count, chan), jnp.float32)
    live_second = jnp.zeros((count, count, chan), jnp.float32)
    for n in range(count):
        key_live = jnp.where(key_at == n, live[n], key_live)
        live_first = jnp.where(first_at == n, live[n], live_first)
        live_second = jnp.where(second_at == n, live[n], live_second)
    key_shift = (key_live - 1.0) * MASK_SHIFT
    pair_mask = (live_first * live_second).reshape(pairs, chan)
    lane_head = lax.broadcasted_iota(jnp.int32, (pairs, width), 1) // size

    def heads_apart(values):
        return jnp.concatenate(
            [jnp.where(lane_head == h, values, 0.0) for h in range(head_count)], axis=0
        )

    def heads_together(values):
        total = jnp.where(lane_head == 0, values[0:pairs], 0.0)
        for h in range(1, head_count):
            total = jnp.where(lane_head == h, values[h * pairs : (h + 1) * pairs], total)
        return total

    def spread_over(values, where):
        return jnp.where(where, values[None], 0.0).reshape(pairs, lanes)

    def fold(values, where):
        return jnp.sum(jnp.where(where, values.reshape(count, count, lanes), 0.0), axis=0)

    for receive in weight_receives:
        receive.wait_recv()

    outs = []
    for t in range(2):
        blocks = []
        for h in range(head_count):
            blocks.append(tri_in_all[h // half, t, :, h % half, :])
        for block in range(4):
            columns = jnp.concatenate(
                [b[:, block * size : (block + 1) * size] for b in blocks], axis=1
            )
            high, low = split(columns)
            wide_hi[t, :, block * width : (block + 1) * width] = high
            wide_lo[t, :, block * width : (block + 1) * width] = low
        bias_rows = jnp.concatenate(
            [tri_bias_all[core, t] for core in range(cores_n)]
            + [jnp.zeros((chan - head_count, chan), jnp.float32)],
            axis=0,
        )
        bias_turned = bias_rows.T
        bias_columns = jnp.concatenate(
            [
                jnp.broadcast_to(bias_turned[:, h : h + 1], (chan, pairs))
                for h in range(head_count)
            ],
            axis=1,
        )
        high, low = split(bias_columns)
        wide_hi[t, :, 4 * width :] = high
        wide_lo[t, :, 4 * width :] = low
        outs.append(
            split(
                jnp.concatenate(
                    [tri_out_all[h // half, t, h % half] for h in range(head_count)], axis=0
                )
            )
        )

    for receive in receives:
        receive.wait_recv()

    left_tiles = []
    right_tiles = []
    for core in range(cores_n):
        for piece in range(pieces):
            base = piece * 2 * OPC
            left_tiles.append(
                jnp.concatenate(
                    [block_all[core, n, count : count + 8, base : base + OPC] for n in range(count)], axis=1
                )
            )
            right_tiles.append(
                jnp.concatenate(
                    [
                        block_all[core, n, count : count + 8, base + OPC : base + 2 * OPC]
                        for n in range(count)
                    ],
                    axis=1,
                )
            )
    left = jnp.concatenate(left_tiles, axis=0)
    right = jnp.concatenate(right_tiles, axis=0)
    mixed = pair_dot(split(right), split(left), TN)
    for block in range(mixed_v.shape[0]):
        mixed_v[block] = mixed[:, block * chan : (block + 1) * chan]
    strips = [[] for _ in range(count)]
    for q in range(OPC):
        for block in range(mixed_v.shape[0]):
            tile = mixed_v[block, pl.ds(q, count, stride=OPC), :]
            for n in range(chan // OPC):
                strips[block * (chan // OPC) + n].append(tile[:, n * OPC : (n + 1) * OPC])
    crossed = jnp.concatenate([jnp.concatenate(s, axis=1) for s in strips], axis=0)
    summed = pair_dot(split(crossed), (table_hi[...], table_lo[...]), NN)
    mask_rows = jnp.concatenate(
        [block_all[my_core, n, count + 8 : count + 9] for n in range(count)], axis=0
    )
    counts = jnp.sum(mask_rows[:, None, :] * mask_rows[None, :, :], axis=-1, keepdims=True)
    acts = jnp.concatenate([block_all[my_core, n, 0:count] for n in range(count)], axis=0)
    pair_one = acts + summed / counts.reshape(pairs, 1)

    def turn(values):
        turn_v[...] = values
        return jnp.concatenate(
            [turn_v[pl.ds(n, count, stride=count), :] for n in range(count)], axis=0
        )

    scale = size ** (-0.5)

    def forward(x, t):
        gain = tri_gain_v[t : t + 1]
        hat, inverse = standardize(x)
        weights = (wide_hi[t], wide_lo[t])
        projected = pair_dot(split(hat * gain), weights, NN)
        query = projected[:, 0:width] * scale
        key = split(projected[:, width : 2 * width])
        value = split(projected[:, 2 * width : 3 * width])
        gate = jax.nn.sigmoid(projected[:, 3 * width : 4 * width])
        bias = fold(projected[:, 4 * width :], at_second)
        query_apart = split(heads_apart(query))
        logits = fold(pair_dot(key, query_apart, NT), at_first) + bias + key_shift
        top = jnp.max(logits, axis=0, keepdims=True)
        exps = jnp.exp(logits - top)
        probs = exps / jnp.sum(exps, axis=0, keepdims=True)
        probs_wide = split(spread_over(probs, at_first))
        attended = heads_together(pair_dot(probs_wide, value, TN))
        update = pair_dot(split(gate * attended), outs[t], NN)
        saved = (hat, inverse, gain, weights, key, value, gate, query_apart, probs, probs_wide, attended)
        return (x + update * pair_mask, saved)

    def gated_of(grad, t):
        return pair_dot(split(grad * pair_mask), outs[t], NT)

    def backward(grad, d_gated, t, saved):
        hat, inverse, gain, weights, key, value, gate, query_apart, probs, probs_wide, attended = saved
        d_gate = d_gated * attended * gate * (1.0 - gate)
        d_apart = split(heads_apart(d_gated * gate))
        d_probs = fold(pair_dot(value, d_apart, NT), at_first)
        d_value = pair_dot(probs_wide, d_apart, NN)
        d_logits = probs * (d_probs - jnp.sum(probs * d_probs, axis=0, keepdims=True))
        d_wide = split(spread_over(d_logits, at_first))
        d_key = pair_dot(d_wide, query_apart, NN)
        d_query = heads_together(pair_dot(d_wide, key, TN)) * scale
        d_bias = spread_over(d_logits, at_second)

        def through(values, start, stop):
            return pair_dot(split(values), (weights[0][:, start:stop], weights[1][:, start:stop]), NT)

        early = through(jnp.concatenate([d_value, d_gate], axis=1), 2 * width, 4 * width)
        middle = through(d_bias, 4 * width, 4 * width + lanes)
        late = through(jnp.concatenate([d_query, d_key], axis=1), 0, 2 * width)
        d_normed = (early + middle + late) * gain
        mean_d = jnp.mean(d_normed, axis=-1, keepdims=True)
        mean_dh = jnp.mean(d_normed * hat, axis=-1, keepdims=True)
        return grad + inverse * (d_normed - mean_d - hat * mean_dh)

    pair_two, saved_start = forward(pair_one, 0)
    for receive in cot_receives:
        receive.wait_recv()
    cot = jnp.concatenate([cot_all[:, n, :] for n in range(count)], axis=0)
    cot_gated = gated_of(cot, 1)
    turned, saved_end = forward(turn(pair_two), 1)
    turn_v[...] = turned
    out_ref[0] = turn_v[pl.ds(me, count, stride=count), :]

    grad_two = turn(backward(cot, cot_gated, 1, saved_end))
    turn_v[...] = backward(grad_two, gated_of(grad_two, 0), 0, saved_start)
    out_ref[1] = turn_v[pl.ds(pl.multiple_of(me * count, count), count), :]

    for copy in sends:
        copy.wait_send()


def fused_body(shape, args):
    (
        pair_acts,
        alignment,
        align_mask,
        residue_mask,
        align_gain,
        outer_in,
        outer_out,
        tri_gain,
        tri_in,
        tri_bias,
        tri_out,
        pair_cotangent,
    ) = args
    rows_n, heads_n, cores_n = shape["row"], shape["head"], shape["br"]
    count = rows_n * heads_n
    chan = pair_acts.shape[-1]
    seqs = alignment.shape[0]
    half, size = tri_in.shape[2], tri_in.shape[3] // 4
    head_count = half * cores_n
    lanes = head_count * count * count
    wide = 4 * head_count * size + lanes
    others = count * cores_n
    f32, b16 = jnp.float32, jnp.bfloat16
    anywhere = pl.BlockSpec(memory_space=pl.ANY)
    here = pl.BlockSpec(memory_space=pltpu.VMEM)
    dma = pltpu.SemaphoreType.DMA
    scratch = [
        pltpu.VMEM((cores_n, count, count + 16, chan), f32),
        pltpu.VMEM((count, count, chan), f32),
        pltpu.VMEM(alignment.shape, f32),
        pltpu.VMEM(align_mask.shape[::-1], jnp.int32),
        pltpu.VMEM((1, align_gain.shape[0]), f32),
        pltpu.VMEM(outer_in.shape[::-1], f32),
        pltpu.VMEM(outer_out.shape, f32),
        pltpu.VMEM(tri_gain.shape, f32),
        pltpu.VMEM((cores_n,) + tri_in.shape, f32),
        pltpu.VMEM((cores_n, 2, half, chan), f32),
        pltpu.VMEM((cores_n,) + tri_out.shape, f32),
        pltpu.VMEM(outer_out.shape, b16),
        pltpu.VMEM(outer_out.shape, b16),
        pltpu.VMEM((2, chan, wide), b16),
        pltpu.VMEM((2, chan, wide), b16),
        pltpu.VMEM((count * count, chan), f32),
        pltpu.VMEM((count * OPC // chan, count * OPC, chan), f32),
        dma((11,)),
        dma((others,)),
        dma((cores_n, count)),
        dma((others,)),
        dma((count,)),
        dma((3, cores_n)),
        dma((3, cores_n)),
    ]
    both = pl.pallas_call(
        functools.partial(fused_kernel, (rows_n, heads_n, cores_n)),
        out_shape=pltpu.VMEM((2,) + pair_acts.shape[1:], f32),
        in_specs=[pl.BlockSpec(memory_space=pltpu.SMEM)] + [anywhere] * 11,
        out_specs=here,
        scratch_shapes=scratch,
        compiler_params=pltpu.CompilerParams(collective_id=0, has_side_effects=True),
    )(
        residue_mask,
        pair_acts,
        alignment,
        align_mask.T,
        align_gain[None],
        outer_in.T,
        outer_out,
        tri_gain,
        tri_in,
        jnp.swapaxes(tri_bias, 1, 2),
        tri_out,
        pair_cotangent,
    )
    return (both[0:1], both[1:2])


def dispatch(shape, *args):
    pair_acts, alignment, align_mask, tri_in = args[0], args[1], args[2], args[8]
    count = pair_acts.shape[1]
    head_count = tri_in.shape[2] * shape["br"]
    chan = pair_acts.shape[-1]
    fits = (
        pair_acts.shape[0] == 1
        and alignment.shape[1] == 1
        and count % 8 == 0
        and alignment.shape[0] // 8 * 2 * OPC == chan
        and align_mask.shape[0] <= chan
        and head_count * (tri_in.shape[3] // 4) == chan
        and head_count * count**4 * 4 <= FUSED_BYTES
    )
    return fused_body(shape, args) if fits else spread_body(*args)


def solution(mesh):
    in_specs = (
        P(("grp", "row", "head"), None, None),
        P(("grp", "br"), ("row", "head"), None),
        P("grp", ("row", "head")),
        P("grp"),
        P(),
        P(),
        P(),
        P(),
        P(None, None, "br", None),
        P(None, None, "br"),
        P(None, "br", None, None),
        P(("grp", "row", "head"), None, None),
    )
    out_specs = (P(("grp", "row", "head"), None, None), P(("grp", "row", "head"), None, None))
    return jax.shard_map(functools.partial(dispatch, dict(mesh.shape)), mesh=mesh, in_specs=in_specs, out_specs=out_specs, check_vma=False)
```
